512 devices in a mesh: row: 16 (over z_hi, x, core), col: 32 (over z_lo, y).
Axes of the slice: x: 4, y: 8, z: 8 (z_hi: 2, z_lo: 4; z = z_hi * 4 + z_lo), core: 2. Of those that a mesh axis runs over, the one named last changes fastest.
Arguments:
- object_slices: bfloat16 [2, 2, 4096, 8192], P(None, None, 'row', 'col'), may hold values from -4 to 4
- probe_wave_parts: float32 [32, 2, 256, 256], P('col'), may hold values from -4 to 4
- prop_phase: float32 [256, 256], replicated, may hold values from -3.140625 to 3.140625
- measured: float32 [2048, 256, 256], P(('row', 'col')), may hold values from 0 to 2
- positions: int32 [2048, 2], P(('row', 'col')), may hold values from 0 to 255
Outputs:
- grad_object: float32 [2, 2, 4096, 8192], P(None, None, 'row', 'col')
- probe_grad: float32 [32, 2, 256, 256], P('col')
The draws below stay inside these ranges and needn't reach their ends.
Inputs may be any that keep to these rules, and one draw needn't show every extreme that they name: Each device holds only positions inside its own tile; a window covers the tile's rows from its centre row - 128 to centre row + 127, likewise columns.
All inputs are finite; a program needn't handle non-finite values.
Results may differ from the reference program's by a relative error of at most 0.015.
Values may be sent and summed in bfloat16 or wider, within the bound.
A program may use at most 64 MiB of HBM per device.

```python
import math
import jax
import jax.numpy as jnp
from jax import lax

WIN = 256
SCAN_PER_UNIT = 4
TILE = 256
HALF = 128
ROWS = 4096
COLS = 8192
NPOS = 2048
N_ROW = 16
N_COL = 32


def set_ends(entries, rng, low, largest):
    extent = entries.shape
    place = [jax.random.randint(jax.random.fold_in(rng, axis), (), 0, extent[axis]) for axis in range(len(extent))]
    entries = entries.at[tuple(place)].set(low)
    longest = extent.index(max(extent))
    place[longest] = (place[longest] + 1) % extent[longest]
    return entries.at[tuple(place)].set(largest)


def levels(rng, dims, split, smallest, largest):
    gain, own = 1.0, jax.random.fold_in(rng, 6)
    for position, parts in split:
        heights = jnp.exp(jax.random.uniform(jax.random.fold_in(own, position), (parts,), jnp.float32, smallest / len(split), largest / len(split)))
        gain = gain * jnp.repeat(heights, dims[position] // parts).reshape([-1 if axis == position else 1 for axis in range(len(dims))])
    return gain


def noise(rng, extent, spread, bound, shards=(), kind=jnp.bfloat16):
    values = jax.random.normal(rng, extent, jnp.float32) * spread
    if len(shards) > 0:
        values = levels(rng, extent, shards, -0.22, 0.18) * values
    return jnp.clip(values, min=-bound, max=bound).astype(kind)


def setup_inputs(seed: int = 0) -> dict:
    arg_keys = jax.random.split(jax.random.key(seed), 6)
    return {
        "object_slices": noise(arg_keys[0], (2, 2, ROWS, COLS), 0.7, 4.0, ((2, 16), (3, 32))),
        "probe_wave_parts": noise(arg_keys[1], (N_COL, 2, WIN, WIN), 0.7, 4.0, ((0, 32),), jnp.float32),
        "prop_phase": jnp.clip(jax.random.uniform(arg_keys[2], (WIN, WIN), jnp.float32, -3.140625, 3.140625), -3.140625, 3.140625),
        "measured": jnp.clip(2.0 * jax.random.uniform(arg_keys[3], (NPOS, WIN, WIN), jnp.float32) ** levels(arg_keys[3], (NPOS, WIN, WIN), ((0, 512),), -0.2, 0.2), 0.0, 2.0),
        "positions": set_ends(jax.random.randint(arg_keys[4], (NPOS, 2), 0, TILE), jax.random.fold_in(arg_keys[4], 1), 0, TILE - 1).astype(jnp.int32),
    }


def dft_tables(length, direction):
    numbers = jnp.arange(length, dtype=jnp.int32)
    phase_int = numbers[:, None] * numbers[None, :] % length
    angles = 2.0 * math.pi / length * phase_int.astype(jnp.float32)
    cosine = jnp.cos(angles) / math.sqrt(length)
    sine_part = direction * jnp.sin(angles) / math.sqrt(length)
    matrix = jnp.stack([jnp.stack([cosine, sine_part]), jnp.stack([-sine_part, cosine])])
    return matrix.astype(jnp.bfloat16)

def transform(wave_in, matrix):
    matrix32 = matrix.astype(jnp.float32)
    rounded = lax.optimization_barrier(wave_in.astype(jnp.bfloat16)).astype(jnp.float32)
    halfway = jnp.einsum('pqab,nqbc->npac', matrix32, rounded)
    halfway = lax.optimization_barrier(halfway.astype(jnp.bfloat16)).astype(jnp.float32)
    return jnp.einsum('nqac,pqcd->npad', halfway, matrix32)

def complex_mul(former, latter):
    real_part = former[:, 0] * latter[:, 0] - former[:, 1] * latter[:, 1]
    imag_part = former[:, 0] * latter[:, 1] + former[:, 1] * latter[:, 0]
    return jnp.stack([real_part, imag_part], axis=1)

def conj_mul(former, latter):
    real_part = former[:, 0] * latter[:, 0] + former[:, 1] * latter[:, 1]
    imag_part = former[:, 0] * latter[:, 1] - former[:, 1] * latter[:, 0]
    return jnp.stack([real_part, imag_part], axis=1)

def gradient_per_window(extended, window_corners, probe_wave_parts, fresnel_propagator, measured, forward_transform, inverse_transform):
    zero_index = jnp.zeros((), jnp.int32)
    win_size = probe_wave_parts.shape[1]
    windows = jax.vmap(lambda start_pair: lax.dynamic_slice(extended, (zero_index, zero_index, start_pair[0], start_pair[1]), (2, 2, win_size, win_size)))(window_corners)
    windows = windows.astype(jnp.float32)
    slice_one = windows[:, 0]
    slice_two = windows[:, 1]
    first_exit = complex_mul(probe_wave_parts[None], slice_one)
    spectrum = complex_mul(fresnel_propagator[None], transform(first_exit, forward_transform))
    wavefield = transform(spectrum, inverse_transform)
    detector = transform(complex_mul(wavefield, slice_two), forward_transform)
    intensity = detector[:, 0] * detector[:, 0] + detector[:, 1] * detector[:, 1]
    misfit = (intensity - measured)[:, None] * detector
    back_two = transform(misfit, inverse_transform)
    grad_second = conj_mul(wavefield, back_two)
    back_spec = transform(conj_mul(slice_two, back_two), forward_transform)
    back_one = transform(conj_mul(fresnel_propagator[None], back_spec), inverse_transform)
    grad_first = conj_mul(probe_wave_parts[None], back_one)
    probe_sum = lax.optimization_barrier(jnp.sum(conj_mul(slice_one, back_one), axis=0))
    illumination = lax.optimization_barrier(jnp.sum(slice_one[:, 0] * slice_one[:, 0] + slice_one[:, 1] * slice_one[:, 1], axis=0))
    return (jnp.stack([grad_first, grad_second], axis=1), probe_sum, illumination)

def add_windows(total, window_gradient_stack, window_corners):
    zero_index = jnp.zeros((), jnp.int32)
    win_size = window_gradient_stack.shape[-1]

    def place_one(number, current):
        start_pair = window_corners[number]
        where = (zero_index, zero_index, start_pair[0], start_pair[1])
        present = lax.dynamic_slice(current, where, (2, 2, win_size, win_size))
        return lax.dynamic_update_slice(current, present + window_gradient_stack[number], where)
    return lax.fori_loop(0, window_gradient_stack.shape[0], place_one, total)

def reference(object_slices, probe_wave_parts, prop_phase, measured, positions):
    forward_transform = dft_tables(WIN, 1.0)
    inverse_transform = dft_tables(WIN, -1.0)
    padded_object = jnp.pad(object_slices, ((0, 0), (0, 0), (HALF, HALF), (HALF, HALF)))
    fresnel_propagator = jnp.stack([jnp.cos(prop_phase), jnp.sin(prop_phase)])

    def device_step(carry, unit_index):
        grad_pad, probe_sum, illum_sum = carry
        tile_row = unit_index // N_COL
        tile_col = unit_index % N_COL
        local_pos = lax.dynamic_slice_in_dim(positions, (unit_index * SCAN_PER_UNIT).astype(jnp.int32), SCAN_PER_UNIT, 0)
        local_measured_data = lax.dynamic_slice_in_dim(measured, (unit_index * SCAN_PER_UNIT).astype(jnp.int32), SCAN_PER_UNIT, 0)
        offset = jnp.stack([tile_row * TILE, tile_col * TILE]).astype(jnp.int32)
        window_corners = (local_pos + offset[None]).astype(jnp.int32)
        probe_here = lax.dynamic_index_in_dim(probe_wave_parts, tile_col, 0, keepdims=False)
        window_gradient_stack, probe_piece, illumination_piece = gradient_per_window(padded_object, window_corners, probe_here, fresnel_propagator, local_measured_data, forward_transform, inverse_transform)
        grad_pad = add_windows(grad_pad, window_gradient_stack, window_corners)
        probe_now = lax.dynamic_index_in_dim(probe_sum, tile_col, 0, keepdims=False)
        probe_sum = lax.dynamic_update_index_in_dim(probe_sum, probe_now + probe_piece, tile_col, 0)
        illum_now = lax.dynamic_index_in_dim(illum_sum, tile_col, 0, keepdims=False)
        illum_sum = lax.dynamic_update_index_in_dim(illum_sum, illum_now + illumination_piece, tile_col, 0)
        return ((grad_pad, probe_sum, illum_sum), None)
    initial = (jnp.zeros(padded_object.shape, jnp.float32), jnp.zeros((N_COL, 2, WIN, WIN), jnp.float32), jnp.zeros((N_COL, WIN, WIN), jnp.float32))
    (grad_pad, probe_sum, illum_sum), _ = lax.scan(device_step, initial, jnp.arange(N_ROW * N_COL, dtype=jnp.int32))
    grad_object = grad_pad[:, :, HALF:HALF + ROWS, HALF:HALF + COLS]
    probe_grad = probe_sum / jnp.sqrt(illum_sum + 1e-06)[:, None]
    return (grad_object, probe_grad)
```

```python
import functools

import jax
import jax.numpy as jnp
import numpy as np
from jax import lax
from jax.experimental import pallas as pl
from jax.experimental.pallas import tpu as pltpu
from jax.sharding import PartitionSpec as P

W = 256
H = 128
NP = 4
RC = 128
F32, BF16 = jnp.float32, jnp.bfloat16
MESH = pl.DeviceIdType.MESH
AROUND = ((-1, 0), (1, 0), (-1, -1), (-1, 1), (1, -1), (1, 1), (0, -1), (0, 1))
CHUNKS = [slice(i, i + RC) for i in range(0, W, RC)]
XS, ZS = 4, 2


def half_of(step):
    return {-1: slice(0, H), 0: slice(0, W), 1: slice(H, W)}[step]


def rim_of(step):
    return {-1: slice(3 * H, 4 * H), 0: slice(H, 3 * H), 1: slice(0, H)}[step]


def spot_of(step):
    return {-1: slice(0, H), 0: slice(H, 3 * H), 1: slice(3 * H, 4 * H)}[step]


def moved(q, by):
    return slice(q.start + by, q.stop + by)


def kernel(
    n_row, n_col,
    pos, obj, probe, phase, meas_in, cs,
    center, probe_grad,
    fwd_t, inv_t, prop, u, v, h, ext, pr, wave, g, sums, meas,
    out_row, out_col, got_row, got_col,
    core_out, core_got, x_out, x_got, z_out, z_got, fin,
    local_sem, halo_send, halo_recv, fold_send, fold_recv, sum_send, sum_recv,
):
    r, c = lax.axis_index("row"), lax.axis_index("col")
    core = lax.rem(r, 2)
    xi = lax.rem(r // 2, XS)
    zi = r // (2 * XS)

    def inside(dr, dc):
        ok = None
        for idx, step, count in ((r, dr, n_row), (c, dc, n_col)):
            if step:
                here = (idx > 0) if step < 0 else (idx < count - 1)
                ok = here if ok is None else ok & here
        return ok

    def row_at(z, x, k):
        return (z * XS + x) * 2 + k

    mates = [(row_at(zi, xi, 1 - core), c), (row_at(1 - zi, xi, core), c)]
    mates += [(row_at(zi, lax.rem(xi + d, XS), core), c) for d in range(1, XS)]

    barrier = pltpu.get_barrier_semaphore()
    for dr, dc in AROUND:
        @pl.when(inside(dr, dc))
        def _():
            pl.semaphore_signal(barrier, inc=1, device_id=(r + dr, c + dc), device_id_type=MESH)
    for mate in mates[1:]:
        pl.semaphore_signal(barrier, inc=1, device_id=mate, device_id_type=MESH)
    own = pltpu.make_async_copy(obj, ext.at[:, pl.ds(H, W), pl.ds(H, W)], local_sem.at[0])
    own.start()
    load = pltpu.make_async_copy(meas_in, meas, local_sem.at[1])
    load.start()
    peers = jnp.int32(len(mates) - 1)
    for dr, dc in AROUND:
        peers = peers + inside(dr, dc).astype(jnp.int32)
    pl.semaphore_wait(barrier, peers)

    def halo(s, k):
        dr, dc = AROUND[k]
        a, b, e, f = half_of(dr), half_of(dc), rim_of(dr), rim_of(dc)
        return pltpu.make_async_remote_copy(
            src_ref=obj.at[pl.ds(2 * s, 2), a, b],
            dst_ref=ext.at[pl.ds(2 * s, 2), e, f],
            send_sem=halo_send.at[s, k],
            recv_sem=halo_recv.at[s, k],
            device_id=(r + dr, c + dc),
            device_id_type=MESH,
        )

    def fold(s, k):
        dr, dc = AROUND[k]
        if dr:
            i = 0 if dr < 0 else 1
            place = (i, pl.ds(2 * s, 2), slice(None), spot_of(dc))
            src, dst = out_row.at[place], got_row.at[place]
        else:
            i = 0 if dc < 0 else 1
            place = (i, pl.ds(2 * s, 2))
            src, dst = out_col.at[place], got_col.at[place]
        return pltpu.make_async_remote_copy(
            src_ref=src, dst_ref=dst, send_sem=fold_send.at[s, k], recv_sem=fold_recv.at[s, k],
            device_id=(r + dr, c + dc), device_id_type=MESH,
        )

    def to_mate(src, dst, i, mate):
        return pltpu.make_async_remote_copy(
            src_ref=src, dst_ref=dst, send_sem=sum_send.at[i], recv_sem=sum_recv.at[i],
            device_id=mate, device_id_type=MESH,
        )

    def start(make, s):
        for k, (dr, dc) in enumerate(AROUND):
            @pl.when(inside(dr, dc))
            def _():
                make(s, k).start()

    def sent(make, s):
        for k, (dr, dc) in enumerate(AROUND):
            @pl.when(inside(dr, dc))
            def _():
                make(s, k).wait_send()

    def arrived(make, s):
        for k, (dr, dc) in enumerate(AROUND):
            @pl.when(inside(-dr, -dc))
            def _():
                make(s, k).wait_recv()

    start(halo, 0)
    start(halo, 1)

    for dr, dc in AROUND:
        @pl.when(jnp.logical_not(inside(-dr, -dc)))
        def _():
            e, f = rim_of(dr), rim_of(dc)
            ext[:, e, f] = jnp.zeros((4, e.stop - e.start, f.stop - f.start), BF16)

    cos_t, sin_t = cs[0], cs[1]
    for t, sgn in ((fwd_t, 1), (inv_t, -1)):
        t[0:W, 0:W] = cos_t
        t[W:, W:] = cos_t
        t[0:W, W:] = sin_t if sgn > 0 else -sin_t
        t[W:, 0:W] = -sin_t if sgn > 0 else sin_t
    for q in CHUNKS:
        prop[0, q] = jnp.cos(phase[q])
        prop[1, q] = jnp.sin(phase[q])
    sums[...] = jnp.zeros_like(sums)

    def rolled(n, _):
        for k in range(2):
            pr[n, k] = pltpu.roll(pltpu.roll(probe[k], pos[n, 0], 0), pos[n, 1], 1)
        return 0
    lax.fori_loop(0, NP, rolled, 0)

    def transform(src, lt, rt, epilogue):
        half = jnp.dot(lt[...], src, preferred_element_type=F32)
        h[:, 0:W] = half[0:W].astype(BF16)
        h[:, W:] = half[W:].astype(BF16)
        for q in CHUNKS:
            o = jnp.dot(h[q, :], rt[...], preferred_element_type=F32)
            epilogue(q, o[:, 0:W], o[:, W:])

    def put(q, re, im):
        u[q, :] = re.astype(BF16)
        u[moved(q, W), :] = im.astype(BF16)

    def picker(n):
        at, to = pos[n, 0], pos[n, 1]
        col = lax.broadcasted_iota(jnp.int32, (RC, W), 1) >= to
        row = lax.broadcasted_iota(jnp.int32, (RC, W), 0)

        def pick(plane, q):
            q2 = moved(q, W)
            a = jnp.where(col, ext[plane, q, 0:W].astype(F32), ext[plane, q, W:].astype(F32))
            b = jnp.where(col, ext[plane, q2, 0:W].astype(F32), ext[plane, q2, W:].astype(F32))
            return jnp.where(row + q.start >= at, a, b)
        return pick

    def back(x, n):
        return pltpu.roll(pltpu.roll(x, W - pos[n, 0], 0), W - pos[n, 1], 1)

    own.wait()
    arrived(halo, 0)

    def first(n, _):
        pick = picker(n)
        for q in CHUNKS:
            a, b = pick(0, q), pick(1, q)
            p, t = pr[n, 0, q], pr[n, 1, q]
            put(q, p * a - t * b, p * b + t * a)
            g[n, 0, q] = a * a + b * b
        sums[2] += back(g[n, 0], n)

        def e1(q, re, im):
            p, t = prop[0, q], prop[1, q]
            put(q, p * re - t * im, p * im + t * re)
        transform(u[...], fwd_t, inv_t, e1)

        def e2(q, re, im):
            wave[n, 0, q] = re
            wave[n, 1, q] = im
        transform(u[...], inv_t, fwd_t, e2)
        return 0
    lax.fori_loop(0, NP, first, 0)

    load.wait()
    arrived(halo, 1)

    def second(n, _):
        pick = picker(n)
        for q in CHUNKS:
            a, b = pick(2, q), pick(3, q)
            re, im = wave[n, 0, q], wave[n, 1, q]
            put(q, re * a - im * b, re * b + im * a)

        def e3(q, re, im):
            res = re * re + im * im - meas[n, q]
            put(q, res * re, res * im)
        transform(u[...], fwd_t, inv_t, e3)

        def e4(q, re, im):
            wr, wi = wave[n, 0, q], wave[n, 1, q]
            g[n, 2, q] = wr * re + wi * im
            g[n, 3, q] = wr * im - wi * re
            a, b = pick(2, q), pick(3, q)
            v[n, q] = (a * re + b * im).astype(BF16)
            v[n, moved(q, W)] = (a * im - b * re).astype(BF16)
        transform(u[...], inv_t, fwd_t, e4)
        return 0
    lax.fori_loop(0, NP, second, 0)

    def total(plane, q, a, b, cols):
        acc = None
        for n in range(NP):
            row = lax.broadcasted_iota(jnp.int32, (q.stop - q.start, H), 0) + q.start
            col = lax.broadcasted_iota(jnp.int32, (q.stop - q.start, H), 1) + cols.start
            m = (row >= pos[n, 0]) if a == 0 else (row < pos[n, 0])
            m = m & ((col >= pos[n, 1]) if b == 0 else (col < pos[n, 1]))
            part = jnp.where(m, g[n, plane, q, cols], 0.0)
            acc = part if acc is None else acc + part
        return acc

    lo, hi = slice(0, H), slice(H, W)

    def outer(plane, _):
        for j in range(4):
            out_row[0, plane, :, j * H:(j + 1) * H] = total(plane, lo, 0, j // 2, (lo, hi)[j % 2]).astype(BF16)
            out_row[1, plane, :, j * H:(j + 1) * H] = total(plane, hi, 1, j // 2, (lo, hi)[j % 2]).astype(BF16)
        for i, q in enumerate((hi, lo)):
            rows = slice(i * H, (i + 1) * H)
            out_col[0, plane, rows] = total(plane, q, i, 0, lo).astype(BF16)
            out_col[1, plane, rows] = total(plane, q, i, 1, hi).astype(BF16)
        return 0

    def inner(plane, _):
        for i, q in enumerate((hi, lo)):
            rows = slice(i * H, (i + 1) * H)
            center[plane, rows, 0:H] = total(plane, q, i, 0, hi)
            center[plane, rows, H:] = total(plane, q, i, 1, lo)
        return 0

    def add_fold(s, k):
        dr, dc = AROUND[k]
        e = half_of(-dr)
        f = half_of(-dc)

        @pl.when(inside(-dr, -dc))
        def _():
            fold(s, k).wait_recv()
            for plane in (2 * s, 2 * s + 1):
                if dr:
                    got = got_row[0 if dr < 0 else 1, plane, :, spot_of(dc)]
                else:
                    got = got_col[0 if dc < 0 else 1, plane]
                center[plane, e, f] += got.astype(F32)

    lax.fori_loop(2, 4, outer, 0)
    start(fold, 1)

    def third(n, _):
        def e5(q, re, im):
            p, t = prop[0, q], prop[1, q]
            put(q, p * re + t * im, p * im - t * re)
        transform(v[n], fwd_t, inv_t, e5)
        pick = picker(n)

        def e6(q, re, im):
            p, t = pr[n, 0, q], pr[n, 1, q]
            g[n, 0, q] = p * re + t * im
            g[n, 1, q] = p * im - t * re
            a, b = pick(0, q), pick(1, q)
            wave[n, 0, q] = a * re + b * im
            wave[n, 1, q] = a * im - b * re
        transform(u[...], inv_t, fwd_t, e6)
        sums[0] += back(wave[n, 0], n)
        sums[1] += back(wave[n, 1], n)
        return 0
    lax.fori_loop(0, NP, third, 0)

    mine = pl.ds(pl.multiple_of(core * H, H), H)
    other = pl.ds(pl.multiple_of((1 - core) * H, H), H)
    core_out[...] = sums[:, other].astype(BF16)
    swap = to_mate(core_out, core_got, 0, mates[0])
    swap.start()
    lax.fori_loop(0, 2, outer, 0)
    start(fold, 0)

    Q = H // XS
    swap.wait()
    sums[:, mine] = sums[:, mine] + core_got[...].astype(F32)
    spread = []
    for d in range(1, XS):
        at = pl.multiple_of(core * H + lax.rem(xi + d, XS) * Q, Q)
        x_out[d - 1] = sums[:, pl.ds(at, Q)].astype(BF16)
        cp = to_mate(x_out.at[d - 1], x_got.at[d - 1], d, mates[1 + d])
        cp.start()
        spread.append(cp)
    lax.fori_loop(2, 4, inner, 0)
    lax.fori_loop(0, 2, inner, 0)
    acc = sums[:, pl.ds(pl.multiple_of(core * H + xi * Q, Q), Q)]
    for d in range(1, XS):
        spread[d - 1].wait()
        acc = acc + x_got[d - 1].astype(F32)
    z_out[...] = acc.astype(BF16)
    cross = to_mate(z_out, z_got, XS, mates[1])
    cross.start()
    for k in range(8):
        add_fold(1, k)
    cross.wait()
    tot = z_out[...].astype(F32) + z_got[...].astype(F32)
    scale = 1.0 / jnp.sqrt(tot[2] + 1e-06)
    here = pl.ds(pl.multiple_of(core * H + xi * Q, Q), Q)
    fin[0, here] = (tot[0] * scale).astype(BF16)
    fin[1, here] = (tot[1] * scale).astype(BF16)
    gather = []
    for d in range(1, XS):
        cp = to_mate(fin.at[:, here], fin.at[:, here], XS + d, mates[1 + d])
        cp.start()
        gather.append(cp)
    for d in range(1, XS):
        gather[d - 1].wait()
    last = to_mate(fin.at[:, mine], fin.at[:, mine], 2 * XS, mates[0])
    last.start()
    for k in (6, 7, 0, 1, 2, 3, 4, 5):
        add_fold(0, k)
    last.wait()
    probe_grad[...] = fin[...].astype(F32)
    for s in range(2):
        sent(halo, s)
        sent(fold, s)


def tables():
    k = np.arange(W)
    ang = 2.0 * np.pi * ((k[:, None] * k[None, :]) % W) / W
    both = np.stack([np.cos(ang), np.sin(ang)]) / np.sqrt(W)
    return jnp.asarray(both.astype(np.float32)).astype(BF16)


def on_device(n_row, n_col, object_slices, probe_wave_parts, prop_phase, measured, positions):
    vm = pl.BlockSpec(memory_space=pltpu.VMEM)
    anys = pl.BlockSpec(memory_space=pl.ANY)
    shape = jax.ShapeDtypeStruct
    Q = H // XS
    dma = pltpu.SemaphoreType.DMA
    center, probe_grad = pl.pallas_call(
        functools.partial(kernel, n_row, n_col),
        out_shape=(shape((4, W, W), F32), shape((2, W, W), F32)),
        in_specs=[pl.BlockSpec(memory_space=pltpu.SMEM), anys, vm, vm, anys, vm],
        out_specs=(vm, vm),
        scratch_shapes=[
            pltpu.VMEM((2 * W, 2 * W), BF16), pltpu.VMEM((2 * W, 2 * W), BF16), pltpu.VMEM((2, W, W), F32),
            pltpu.VMEM((2 * W, W), BF16), pltpu.VMEM((NP, 2 * W, W), BF16), pltpu.VMEM((W, 2 * W), BF16),
            pltpu.VMEM((4, 2 * W, 2 * W), BF16), pltpu.VMEM((NP, 2, W, W), F32), pltpu.VMEM((NP, 2, W, W), F32),
            pltpu.VMEM((NP, 4, W, W), F32), pltpu.VMEM((3, W, W), F32), pltpu.VMEM((NP, W, W), F32),
            pltpu.VMEM((2, 4, H, 2 * W), BF16), pltpu.VMEM((2, 4, W, H), BF16),
            pltpu.VMEM((2, 4, H, 2 * W), BF16), pltpu.VMEM((2, 4, W, H), BF16),
            pltpu.VMEM((3, H, W), BF16), pltpu.VMEM((3, H, W), BF16),
            pltpu.VMEM((XS - 1, 3, Q, W), BF16), pltpu.VMEM((XS - 1, 3, Q, W), BF16),
            pltpu.VMEM((3, Q, W), BF16), pltpu.VMEM((3, Q, W), BF16), pltpu.VMEM((2, W, W), BF16),
            dma((2,)), dma((2, 8)), dma((2, 8)), dma((2, 8)), dma((2, 8)), dma((2 * XS + 1,)), dma((2 * XS + 1,)),
        ],
        compiler_params=pltpu.CompilerParams(collective_id=0, has_side_effects=True, vmem_limit_bytes=60 << 20),
    )(positions, object_slices.reshape(4, W, W), probe_wave_parts[0], prop_phase, measured, tables())
    return center.reshape(2, 2, W, W), probe_grad[None]


def solution(mesh):
    return jax.shard_map(
        functools.partial(on_device, mesh.shape["row"], mesh.shape["col"]),
        mesh=mesh,
        in_specs=(
            P(None, None, "row", "col"),
            P("col", None, None, None),
            P(),
            P(("row", "col"), None, None),
            P(("row", "col"), None),
        ),
        out_specs=(P(None, None, "row", "col"), P("col", None, None, None)),
        check_vma=False,
    )
```

```python
import functools

import jax
import jax.numpy as jnp
import numpy as np
from jax import lax
from jax.experimental import pallas as pl
from jax.experimental.pallas import tpu as pltpu
from jax.sharding import PartitionSpec as P

W = 256
H = 128
NP = 4
RC = 128
UNROLL = 4
F32, BF16 = jnp.float32, jnp.bfloat16
MESH = pl.DeviceIdType.MESH
AROUND = ((-1, 0), (1, 0), (-1, -1), (-1, 1), (1, -1), (1, 1), (0, -1), (0, 1))
CHUNKS = [slice(i, i + RC) for i in range(0, W, RC)]
XS, ZS = 4, 2


def half_of(step):
    return {-1: slice(0, H), 0: slice(0, W), 1: slice(H, W)}[step]


def rim_of(step):
    return {-1: slice(3 * H, 4 * H), 0: slice(H, 3 * H), 1: slice(0, H)}[step]


def spot_of(step):
    return {-1: slice(0, H), 0: slice(H, 3 * H), 1: slice(3 * H, 4 * H)}[step]


def moved(q, by):
    return slice(q.start + by, q.stop + by)


def kernel(
    n_row, n_col,
    pos, obj, probe, phase, meas_in, cs,
    grad, fin,
    fwd_t, inv_t, prop, u, v, h, ext, pr, wave, g, sums, meas,
    out_row, out_col, got_row, got_col,
    core_out, core_got, x_out, x_got, z_out, z_got, center,
    local_sem, halo_send, halo_recv, fold_send, fold_recv, sum_send, sum_recv,
):
    r, c = lax.axis_index("row"), lax.axis_index("col")
    core = lax.rem(r, 2)
    xi = lax.rem(r // 2, XS)
    zi = r // (2 * XS)

    def inside(dr, dc):
        ok = None
        for idx, step, count in ((r, dr, n_row), (c, dc, n_col)):
            if step:
                here = (idx > 0) if step < 0 else (idx < count - 1)
                ok = here if ok is None else ok & here
        return ok

    def row_at(z, x, k):
        return (z * XS + x) * 2 + k

    mates = [(row_at(zi, xi, 1 - core), c), (row_at(1 - zi, xi, core), c)]
    mates += [(row_at(zi, lax.rem(xi + d, XS), core), c) for d in range(1, XS)]

    barrier = pltpu.get_barrier_semaphore()
    for dr, dc in AROUND:
        @pl.when(inside(dr, dc))
        def _():
            pl.semaphore_signal(barrier, inc=1, device_id=(r + dr, c + dc), device_id_type=MESH)
    for mate in mates[1:]:
        pl.semaphore_signal(barrier, inc=1, device_id=mate, device_id_type=MESH)
    own = pltpu.make_async_copy(obj, ext.at[:, pl.ds(H, W), pl.ds(H, W)], local_sem.at[0])
    own.start()
    load = pltpu.make_async_copy(meas_in, meas, local_sem.at[1])
    load.start()
    peers = jnp.int32(len(mates) - 1)
    for dr, dc in AROUND:
        peers = peers + inside(dr, dc).astype(jnp.int32)
    pl.semaphore_wait(barrier, peers)

    def halo(s, k):
        dr, dc = AROUND[k]
        a, b, e, f = half_of(dr), half_of(dc), rim_of(dr), rim_of(dc)
        return pltpu.make_async_remote_copy(
            src_ref=obj.at[pl.ds(2 * s, 2), a, b],
            dst_ref=ext.at[pl.ds(2 * s, 2), e, f],
            send_sem=halo_send.at[s, k],
            recv_sem=halo_recv.at[s, k],
            device_id=(r + dr, c + dc),
            device_id_type=MESH,
        )

    def fold(s, k):
        dr, dc = AROUND[k]
        if dr:
            i = 0 if dr < 0 else 1
            place = (i, pl.ds(2 * s, 2), slice(None), spot_of(dc))
            src, dst = out_row.at[place], got_row.at[place]
        else:
            i = 0 if dc < 0 else 1
            place = (i, pl.ds(2 * s, 2))
            src, dst = out_col.at[place], got_col.at[place]
        return pltpu.make_async_remote_copy(
            src_ref=src, dst_ref=dst, send_sem=fold_send.at[s, k], recv_sem=fold_recv.at[s, k],
            device_id=(r + dr, c + dc), device_id_type=MESH,
        )

    def to_mate(src, dst, i, mate):
        return pltpu.make_async_remote_copy(
            src_ref=src, dst_ref=dst, send_sem=sum_send.at[i], recv_sem=sum_recv.at[i],
            device_id=mate, device_id_type=MESH,
        )

    def start(make, s):
        for k, (dr, dc) in enumerate(AROUND):
            @pl.when(inside(dr, dc))
            def _():
                make(s, k).start()

    def sent(make, s):
        for k, (dr, dc) in enumerate(AROUND):
            @pl.when(inside(dr, dc))
            def _():
                make(s, k).wait_send()

    def arrived(make, s):
        for k, (dr, dc) in enumerate(AROUND):
            @pl.when(inside(-dr, -dc))
            def _():
                make(s, k).wait_recv()

    start(halo, 0)
    start(halo, 1)

    for dr, dc in AROUND:
        @pl.when(jnp.logical_not(inside(-dr, -dc)))
        def _():
            e, f = rim_of(dr), rim_of(dc)
            ext[:, e, f] = jnp.zeros((4, e.stop - e.start, f.stop - f.start), BF16)

    cos_t, sin_t = cs[0], cs[1]
    for t, sgn in ((fwd_t, 1), (inv_t, -1)):
        t[0:W, 0:W] = cos_t
        t[W:, W:] = cos_t
        t[0:W, W:] = sin_t if sgn > 0 else -sin_t
        t[W:, 0:W] = -sin_t if sgn > 0 else sin_t
    for q in CHUNKS:
        prop[0, q] = jnp.cos(phase[q])
        prop[1, q] = jnp.sin(phase[q])
    sums[...] = jnp.zeros_like(sums)

    def rolled(n, _):
        for k in range(2):
            pr[n, k] = pltpu.roll(pltpu.roll(probe[k], pos[0, n], 0), pos[1, n], 1)
        return 0
    lax.fori_loop(0, NP, rolled, 0)

    def transform(src, lt, rt, epilogue):
        def run(n):
            half = jnp.dot(lt[...], src[n], preferred_element_type=F32)
            h[n, :, 0:W] = half[0:W].astype(BF16)
            h[n, :, W:] = half[W:].astype(BF16)
            for q in CHUNKS:
                o = jnp.dot(h[n, q, :], rt[...], preferred_element_type=F32)
                epilogue(n, q, o[:, 0:W], o[:, W:])
        return run

    def put(n, q, re, im):
        u[n, q, :] = re.astype(BF16)
        u[n, moved(q, W), :] = im.astype(BF16)

    def pick(n, plane, q):
        col = lax.broadcasted_iota(jnp.int32, (RC, W), 1) >= pos[1, n]
        row = lax.broadcasted_iota(jnp.int32, (RC, W), 0) + q.start >= pos[0, n]
        q2 = moved(q, W)
        a = jnp.where(col, ext[plane, q, 0:W].astype(F32), ext[plane, q, W:].astype(F32))
        b = jnp.where(col, ext[plane, q2, 0:W].astype(F32), ext[plane, q2, W:].astype(F32))
        return jnp.where(row, a, b)

    def sweep(*stages):
        def some(i, _):
            for stage in stages:
                for k in range(UNROLL):
                    stage(i * UNROLL + k)
            return 0
        if UNROLL == NP:
            some(0, 0)
        else:
            lax.fori_loop(0, NP // UNROLL, some, 0)

    def back(x, n):
        return pltpu.roll(pltpu.roll(x, W - pos[0, n], 0), W - pos[1, n], 1)

    own.wait()
    arrived(halo, 0)

    def first_exit(n):
        for q in CHUNKS:
            a, b = pick(n, 0, q), pick(n, 1, q)
            p, t = pr[n, 0, q], pr[n, 1, q]
            put(n, q, p * a - t * b, p * b + t * a)
            g[n, 0, q] = a * a + b * b

    def bright(n):
        sums[2] += back(g[n, 0], n)

    def e1(n, q, re, im):
        p, t = prop[0, q], prop[1, q]
        put(n, q, p * re - t * im, p * im + t * re)

    def e2(n, q, re, im):
        wave[n, 0, q] = re
        wave[n, 1, q] = im
    sweep(first_exit, bright, transform(u, fwd_t, inv_t, e1), transform(u, inv_t, fwd_t, e2))

    load.wait()
    arrived(halo, 1)

    def second_exit(n):
        for q in CHUNKS:
            a, b = pick(n, 2, q), pick(n, 3, q)
            re, im = wave[n, 0, q], wave[n, 1, q]
            put(n, q, re * a - im * b, re * b + im * a)

    def e3(n, q, re, im):
        res = re * re + im * im - meas[n, q]
        put(n, q, res * re, res * im)

    def e4(n, q, re, im):
        wr, wi = wave[n, 0, q], wave[n, 1, q]
        g[n, 2, q] = wr * re + wi * im
        g[n, 3, q] = wr * im - wi * re
        a, b = pick(n, 2, q), pick(n, 3, q)
        v[n, q] = (a * re + b * im).astype(BF16)
        v[n, moved(q, W)] = (a * im - b * re).astype(BF16)
    sweep(second_exit, transform(u, fwd_t, inv_t, e3), transform(u, inv_t, fwd_t, e4))

    def total(plane, q, a, b, cols):
        acc = None
        for n in range(NP):
            row = lax.broadcasted_iota(jnp.int32, (q.stop - q.start, H), 0) + q.start
            col = lax.broadcasted_iota(jnp.int32, (q.stop - q.start, H), 1) + cols.start
            m = (row >= pos[0, n]) if a == 0 else (row < pos[0, n])
            m = m & ((col >= pos[1, n]) if b == 0 else (col < pos[1, n]))
            part = jnp.where(m, g[n, plane, q, cols], 0.0)
            acc = part if acc is None else acc + part
        return acc

    lo, hi = slice(0, H), slice(H, W)

    def outer(plane, _):
        for j in range(4):
            out_row[0, plane, :, j * H:(j + 1) * H] = total(plane, lo, 0, j // 2, (lo, hi)[j % 2]).astype(BF16)
            out_row[1, plane, :, j * H:(j + 1) * H] = total(plane, hi, 1, j // 2, (lo, hi)[j % 2]).astype(BF16)
        for i, q in enumerate((hi, lo)):
            rows = slice(i * H, (i + 1) * H)
            out_col[0, plane, rows] = total(plane, q, i, 0, lo).astype(BF16)
            out_col[1, plane, rows] = total(plane, q, i, 1, hi).astype(BF16)
        return 0

    def inner(plane, _):
        for i, q in enumerate((hi, lo)):
            rows = slice(i * H, (i + 1) * H)
            center[plane, rows, 0:H] = total(plane, q, i, 0, hi)
            center[plane, rows, H:] = total(plane, q, i, 1, lo)
        return 0

    def add_fold(s, k):
        dr, dc = AROUND[k]
        e = half_of(-dr)
        f = half_of(-dc)

        @pl.when(inside(-dr, -dc))
        def _():
            fold(s, k).wait_recv()
            for plane in (2 * s, 2 * s + 1):
                if dr:
                    got = got_row[0 if dr < 0 else 1, plane, :, spot_of(dc)]
                else:
                    got = got_col[0 if dc < 0 else 1, plane]
                center[plane, e, f] += got.astype(F32)

    lax.fori_loop(2, 4, outer, 0)
    start(fold, 1)

    lax.fori_loop(2, 4, inner, 0)

    def e5(n, q, re, im):
        p, t = prop[0, q], prop[1, q]
        put(n, q, p * re + t * im, p * im - t * re)

    def e6(n, q, re, im):
        p, t = pr[n, 0, q], pr[n, 1, q]
        g[n, 0, q] = p * re + t * im
        g[n, 1, q] = p * im - t * re
        a, b = pick(n, 0, q), pick(n, 1, q)
        wave[n, 0, q] = a * re + b * im
        wave[n, 1, q] = a * im - b * re

    def probe_back(n):
        sums[0] += back(wave[n, 0], n)
        sums[1] += back(wave[n, 1], n)
    sweep(transform(v, fwd_t, inv_t, e5), transform(u, inv_t, fwd_t, e6), probe_back)

    mine = pl.ds(pl.multiple_of(core * H, H), H)
    other = pl.ds(pl.multiple_of((1 - core) * H, H), H)
    core_out[...] = sums[:, other].astype(BF16)
    swap = to_mate(core_out, core_got, 0, mates[0])
    swap.start()
    lax.fori_loop(0, 2, outer, 0)
    start(fold, 0)

    Q = H // XS
    swap.wait()
    sums[:, mine] = sums[:, mine] + core_got[...].astype(F32)
    spread = []
    for d in range(1, XS):
        at = pl.multiple_of(core * H + lax.rem(xi + d, XS) * Q, Q)
        x_out[d - 1] = sums[:, pl.ds(at, Q)].astype(BF16)
        cp = to_mate(x_out.at[d - 1], x_got.at[d - 1], d, mates[1 + d])
        cp.start()
        spread.append(cp)
    lax.fori_loop(0, 2, inner, 0)
    acc = sums[:, pl.ds(pl.multiple_of(core * H + xi * Q, Q), Q)]
    for d in range(1, XS):
        spread[d - 1].wait()
        acc = acc + x_got[d - 1].astype(F32)
    z_out[...] = acc.astype(BF16)
    cross = to_mate(z_out, z_got, XS, mates[1])
    cross.start()
    for k in range(8):
        add_fold(1, k)
    cross.wait()
    tot = z_out[...].astype(F32) + z_got[...].astype(F32)
    scale = 1.0 / jnp.sqrt(tot[2] + 1e-06)
    here = pl.ds(pl.multiple_of(core * H + xi * Q, Q), Q)
    fin[0, here] = (tot[0] * scale).astype(BF16)
    fin[1, here] = (tot[1] * scale).astype(BF16)
    gather = []
    for d in range(1, XS):
        cp = to_mate(fin.at[:, here], fin.at[:, here], XS + d, mates[1 + d])
        cp.start()
        gather.append(cp)
    for d in range(1, XS):
        gather[d - 1].wait()
    last = to_mate(fin.at[:, mine], fin.at[:, mine], 2 * XS, mates[0])
    last.start()
    for k in (6, 7, 0, 1, 2, 3, 4, 5):
        add_fold(0, k)
    last.wait()
    for k in range(4):
        grad[k] = center[k].astype(BF16)
    for s in range(2):
        sent(halo, s)
        sent(fold, s)


def tables():
    k = np.arange(W)
    ang = 2.0 * np.pi * ((k[:, None] * k[None, :]) % W) / W
    both = np.stack([np.cos(ang), np.sin(ang)]) / np.sqrt(W)
    return jnp.asarray(both.astype(np.float32)).astype(BF16)


def on_device(n_row, n_col, object_slices, probe_wave_parts, prop_phase, measured, positions):
    vm = pl.BlockSpec(memory_space=pltpu.VMEM)
    anys = pl.BlockSpec(memory_space=pl.ANY)
    shape = jax.ShapeDtypeStruct
    Q = H // XS
    dma = pltpu.SemaphoreType.DMA
    grad, probe_grad = pl.pallas_call(
        functools.partial(kernel, n_row, n_col),
        out_shape=(shape((4, W, W), BF16), shape((2, W, W), BF16)),
        in_specs=[pl.BlockSpec(memory_space=pltpu.SMEM), anys, vm, vm, anys, vm],
        out_specs=(vm, vm),
        scratch_shapes=[
            pltpu.VMEM((2 * W, 2 * W), BF16), pltpu.VMEM((2 * W, 2 * W), BF16), pltpu.VMEM((2, W, W), F32),
            pltpu.VMEM((NP, 2 * W, W), BF16), pltpu.VMEM((NP, 2 * W, W), BF16), pltpu.VMEM((NP, W, 2 * W), BF16),
            pltpu.VMEM((4, 2 * W, 2 * W), BF16), pltpu.VMEM((NP, 2, W, W), F32), pltpu.VMEM((NP, 2, W, W), F32),
            pltpu.VMEM((NP, 4, W, W), F32), pltpu.VMEM((3, W, W), F32), pltpu.VMEM((NP, W, W), F32),
            pltpu.VMEM((2, 4, H, 2 * W), BF16), pltpu.VMEM((2, 4, W, H), BF16),
            pltpu.VMEM((2, 4, H, 2 * W), BF16), pltpu.VMEM((2, 4, W, H), BF16),
            pltpu.VMEM((3, H, W), BF16), pltpu.VMEM((3, H, W), BF16),
            pltpu.VMEM((XS - 1, 3, Q, W), BF16), pltpu.VMEM((XS - 1, 3, Q, W), BF16),
            pltpu.VMEM((3, Q, W), BF16), pltpu.VMEM((3, Q, W), BF16), pltpu.VMEM((4, W, W), F32),
            dma((2,)), dma((2, 8)), dma((2, 8)), dma((2, 8)), dma((2, 8)), dma((2 * XS + 1,)), dma((2 * XS + 1,)),
        ],
        compiler_params=pltpu.CompilerParams(collective_id=0, has_side_effects=True, vmem_limit_bytes=60 << 20),
    )(positions.T, object_slices.reshape(4, W, W), probe_wave_parts[0], prop_phase, measured, tables())
    return grad.reshape(2, 2, W, W).astype(F32), probe_grad[None].astype(F32)


def solution(mesh):
    return jax.shard_map(
        functools.partial(on_device, mesh.shape["row"], mesh.shape["col"]),
        mesh=mesh,
        in_specs=(
            P(None, None, "row", "col"),
            P("col", None, None, None),
            P(),
            P(("row", "col"), None, None),
            P(("row", "col"), None),
        ),
        out_specs=(P(None, None, "row", "col"), P("col", None, None, None)),
        check_vma=False,
    )
```

```python
import functools

import jax
import jax.numpy as jnp
import numpy as np
from jax import lax
from jax.experimental import pallas as pl
from jax.experimental.pallas import tpu as pltpu
from jax.sharding import PartitionSpec as P

W = 256
H = 128
NP = 4
RC = 128
UNROLL = 4
F32, BF16 = jnp.float32, jnp.bfloat16
MESH = pl.DeviceIdType.MESH
AROUND = ((-1, 0), (1, 0), (-1, -1), (-1, 1), (1, -1), (1, 1), (0, -1), (0, 1))
CHUNKS = [slice(i, i + RC) for i in range(0, W, RC)]
XS, ZS = 4, 2
LOOP = 8
TURNS = [(dr, dc) for dc in (-1, 1) for dr in (-1, 1)]


def half_of(step):
    return {-1: slice(0, H), 0: slice(0, W), 1: slice(H, W)}[step]


def rim_of(step):
    return {-1: slice(3 * H, 4 * H), 0: slice(H, 3 * H), 1: slice(0, H)}[step]


def spot_of(step):
    return {-1: slice(0, H), 0: slice(H, 3 * H), 1: slice(3 * H, 4 * H)}[step]


def moved(q, by):
    return slice(q.start + by, q.stop + by)


def kernel(
    n_row, n_col,
    pos, obj, probe, phase, meas_in, cs,
    grad, fin,
    fwd_t, inv_t, prop, u, v, h, ext, pr, wave, g, sums, meas,
    out_row, out_col, got_row, got_col,
    core_out, core_got, x_out, x_got, z_out, z_got, center,
    turned, local_sem, turn_send, turn_recv, halo_send, halo_recv, fold_send, fold_recv, sum_send, sum_recv,
):
    r, c = lax.axis_index("row"), lax.axis_index("col")
    core = lax.rem(r, 2)
    xi = lax.rem(r // 2, XS)
    zi = r // (2 * XS)

    def inside(dr, dc):
        ok = None
        for idx, step, count in ((r, dr, n_row), (c, dc, n_col)):
            if step:
                here = (idx > 0) if step < 0 else (idx < count - 1)
                ok = here if ok is None else ok & here
        return ok

    def col_far(at, step):
        return lax.rem(at, LOOP) == (LOOP - 1 if step > 0 else 0)

    def row_far(at, step):
        return at == (n_row // ZS - 1 if step > 0 else n_row // ZS)

    def bent(row, col, dr, dc):
        return col_far(col, dc) & jnp.logical_not(row_far(row, dr))

    def leaves(k):
        dr, dc = AROUND[k]
        ok = inside(dr, dc)
        return ok & jnp.logical_not(bent(r, c, dr, dc)) if dr and dc else ok

    def lands(k):
        dr, dc = AROUND[k]
        ok = inside(-dr, -dc)
        return ok & jnp.logical_not(bent(r - dr, c - dc, dr, dc)) if dr and dc else ok

    def row_at(z, x, k):
        return (z * XS + x) * 2 + k

    mates = [(row_at(zi, xi, 1 - core), c), (row_at(1 - zi, xi, core), c)]
    mates += [(row_at(zi, lax.rem(xi + d, XS), core), c) for d in range(1, XS)]

    barrier = pltpu.get_barrier_semaphore()
    for dr, dc in AROUND:
        @pl.when(inside(dr, dc))
        def _():
            pl.semaphore_signal(barrier, inc=1, device_id=(r + dr, c + dc), device_id_type=MESH)
    for mate in mates[1:]:
        pl.semaphore_signal(barrier, inc=1, device_id=mate, device_id_type=MESH)
    own = pltpu.make_async_copy(obj, ext.at[:, pl.ds(H, W), pl.ds(H, W)], local_sem.at[0])
    own.start()
    load = pltpu.make_async_copy(meas_in, meas, local_sem.at[1])
    load.start()
    peers = jnp.int32(len(mates) - 1)
    for dr, dc in AROUND:
        peers = peers + inside(dr, dc).astype(jnp.int32)
    pl.semaphore_wait(barrier, peers)

    def halo(s, k):
        dr, dc = AROUND[k]
        a, b, e, f = half_of(dr), half_of(dc), rim_of(dr), rim_of(dc)
        return pltpu.make_async_remote_copy(
            src_ref=obj.at[pl.ds(2 * s, 2), a, b],
            dst_ref=ext.at[pl.ds(2 * s, 2), e, f],
            send_sem=halo_send.at[s, k],
            recv_sem=halo_recv.at[s, k],
            device_id=(r + dr, c + dc),
            device_id_type=MESH,
        )

    def fold(s, k):
        dr, dc = AROUND[k]
        if dr:
            i = 0 if dr < 0 else 1
            place = (i, pl.ds(2 * s, 2), slice(None), spot_of(dc))
            src, dst = out_row.at[place], got_row.at[place]
        else:
            i = 0 if dc < 0 else 1
            place = (i, pl.ds(2 * s, 2))
            src, dst = out_col.at[place], got_col.at[place]
        return pltpu.make_async_remote_copy(
            src_ref=src, dst_ref=dst, send_sem=fold_send.at[s, k], recv_sem=fold_recv.at[s, k],
            device_id=(r + dr, c + dc), device_id_type=MESH,
        )

    def to_mate(src, dst, i, mate):
        return pltpu.make_async_remote_copy(
            src_ref=src, dst_ref=dst, send_sem=sum_send.at[i], recv_sem=sum_recv.at[i],
            device_id=mate, device_id_type=MESH,
        )

    def pass_on(s, t):
        dr, dc = TURNS[t]
        e, f = half_of(dr), rim_of(dc)
        return pltpu.make_async_remote_copy(
            src_ref=ext.at[pl.ds(2 * s, 2), moved(e, H), f],
            dst_ref=ext.at[pl.ds(2 * s, 2), rim_of(dr), f],
            send_sem=turn_send.at[s, t],
            recv_sem=halo_recv.at[s, AROUND.index((dr, dc))],
            device_id=(r + dr, c),
            device_id_type=MESH,
        )

    def turn(s, t):
        dr, dc = TURNS[t]
        k = AROUND.index((dr, dc))
        place = (0 if dr < 0 else 1, pl.ds(2 * s, 2), slice(None), spot_of(dc))
        return pltpu.make_async_remote_copy(
            src_ref=out_row.at[place], dst_ref=turned.at[s, t], send_sem=fold_send.at[s, k], recv_sem=turn_recv.at[s, t],
            device_id=(r + dr, c), device_id_type=MESH,
        )

    def passes(t):
        dr, dc = TURNS[t]
        return inside(0, -dc) & inside(dr, 0) & bent(r, c - dc, dr, dc)

    def gets(t):
        dr, dc = TURNS[t]
        return inside(0, dc) & inside(-dr, 0) & bent(r - dr, c, dr, dc)

    def halo_start(s):
        for k in range(8):
            @pl.when(leaves(k))
            def _():
                halo(s, k).start()

    def halo_turn(s):
        for dc in (-1, 1):
            @pl.when(inside(0, -dc) & col_far(c - dc, dc))
            def _():
                halo(s, AROUND.index((0, dc))).wait_recv()
        for t in range(4):
            @pl.when(passes(t))
            def _():
                pass_on(s, t).start()

    def halo_arrived(s):
        for k, (dr, dc) in enumerate(AROUND):
            ok = inside(-dr, -dc)
            if not dr:
                ok = ok & jnp.logical_not(col_far(c - dc, dc))

            @pl.when(ok)
            def _():
                halo(s, k).wait_recv()

    def halo_sent(s):
        for k in range(8):
            @pl.when(leaves(k))
            def _():
                halo(s, k).wait_send()
        for t in range(4):
            @pl.when(passes(t))
            def _():
                pass_on(s, t).wait_send()

    def fold_start(s):
        for k, (dr, dc) in enumerate(AROUND):
            ok = leaves(k)
            if not dr:
                ok = ok & jnp.logical_not(col_far(c, dc))
            elif dc:
                @pl.when(inside(dr, dc) & bent(r, c, dr, dc))
                def _():
                    turn(s, TURNS.index((dr, dc))).start()

            @pl.when(ok)
            def _():
                fold(s, k).start()

    def fold_turn(s):
        for t, (dr, dc) in enumerate(TURNS):
            @pl.when(gets(t))
            def _():
                turn(s, t).wait_recv()
                rows = half_of(-dr)
                for p in range(2):
                    i = (0 if dc < 0 else 1, 2 * s + p, rows)
                    out_col[i] = (out_col[i].astype(F32) + turned[s, t, p].astype(F32)).astype(BF16)
        for dc in (-1, 1):
            @pl.when(inside(0, dc) & col_far(c, dc))
            def _():
                fold(s, AROUND.index((0, dc))).start()

    def fold_sent(s):
        for k, (dr, dc) in enumerate(AROUND):
            @pl.when(inside(dr, dc))
            def _():
                fold(s, k).wait_send()

    halo_start(0)
    halo_start(1)

    for dr, dc in AROUND:
        @pl.when(jnp.logical_not(inside(-dr, -dc)))
        def _():
            e, f = rim_of(dr), rim_of(dc)
            ext[:, e, f] = jnp.zeros((4, e.stop - e.start, f.stop - f.start), BF16)

    cos_t, sin_t = cs[0], cs[1]
    for t, sgn in ((fwd_t, 1), (inv_t, -1)):
        t[0:W, 0:W] = cos_t
        t[W:, W:] = cos_t
        t[0:W, W:] = sin_t if sgn > 0 else -sin_t
        t[W:, 0:W] = -sin_t if sgn > 0 else sin_t
    for q in CHUNKS:
        prop[0, q] = jnp.cos(phase[q])
        prop[1, q] = jnp.sin(phase[q])
    sums[...] = jnp.zeros_like(sums)

    def rolled(n, _):
        for k in range(2):
            pr[n, k] = pltpu.roll(pltpu.roll(probe[k], pos[0, n], 0), pos[1, n], 1)
        return 0
    lax.fori_loop(0, NP, rolled, 0)

    def transform(src, lt, rt, epilogue):
        def run(n):
            half = jnp.dot(lt[...], src[n], preferred_element_type=F32)
            h[n, :, 0:W] = half[0:W].astype(BF16)
            h[n, :, W:] = half[W:].astype(BF16)
            for q in CHUNKS:
                o = jnp.dot(h[n, q, :], rt[...], preferred_element_type=F32)
                epilogue(n, q, o[:, 0:W], o[:, W:])
        return run

    def put(n, q, re, im):
        u[n, q, :] = re.astype(BF16)
        u[n, moved(q, W), :] = im.astype(BF16)

    def pick(n, plane, q):
        col = lax.broadcasted_iota(jnp.int32, (RC, W), 1) >= pos[1, n]
        row = lax.broadcasted_iota(jnp.int32, (RC, W), 0) + q.start >= pos[0, n]
        q2 = moved(q, W)
        a = jnp.where(col, ext[plane, q, 0:W].astype(F32), ext[plane, q, W:].astype(F32))
        b = jnp.where(col, ext[plane, q2, 0:W].astype(F32), ext[plane, q2, W:].astype(F32))
        return jnp.where(row, a, b)

    def sweep(*stages):
        def some(i, _):
            for stage in stages:
                for k in range(UNROLL):
                    stage(i * UNROLL + k)
            return 0
        if UNROLL == NP:
            some(0, 0)
        else:
            lax.fori_loop(0, NP // UNROLL, some, 0)

    def back(x, n):
        return pltpu.roll(pltpu.roll(x, W - pos[0, n], 0), W - pos[1, n], 1)

    halo_turn(0)
    own.wait()
    halo_arrived(0)

    def first_exit(n):
        for q in CHUNKS:
            a, b = pick(n, 0, q), pick(n, 1, q)
            p, t = pr[n, 0, q], pr[n, 1, q]
            put(n, q, p * a - t * b, p * b + t * a)
            g[n, 0, q] = a * a + b * b

    def bright(n):
        sums[2] += back(g[n, 0], n)

    def e1(n, q, re, im):
        p, t = prop[0, q], prop[1, q]
        put(n, q, p * re - t * im, p * im + t * re)

    def e2(n, q, re, im):
        wave[n, 0, q] = re
        wave[n, 1, q] = im
    sweep(first_exit, bright, transform(u, fwd_t, inv_t, e1))
    halo_turn(1)
    sweep(transform(u, inv_t, fwd_t, e2))

    load.wait()
    halo_arrived(1)

    def second_exit(n):
        for q in CHUNKS:
            a, b = pick(n, 2, q), pick(n, 3, q)
            re, im = wave[n, 0, q], wave[n, 1, q]
            put(n, q, re * a - im * b, re * b + im * a)

    def e3(n, q, re, im):
        res = re * re + im * im - meas[n, q]
        put(n, q, res * re, res * im)

    def e4(n, q, re, im):
        wr, wi = wave[n, 0, q], wave[n, 1, q]
        g[n, 2, q] = wr * re + wi * im
        g[n, 3, q] = wr * im - wi * re
        a, b = pick(n, 2, q), pick(n, 3, q)
        v[n, q] = (a * re + b * im).astype(BF16)
        v[n, moved(q, W)] = (a * im - b * re).astype(BF16)
    sweep(second_exit, transform(u, fwd_t, inv_t, e3), transform(u, inv_t, fwd_t, e4))

    def total(plane, q, a, b, cols):
        acc = None
        for n in range(NP):
            row = lax.broadcasted_iota(jnp.int32, (q.stop - q.start, H), 0) + q.start
            col = lax.broadcasted_iota(jnp.int32, (q.stop - q.start, H), 1) + cols.start
            m = (row >= pos[0, n]) if a == 0 else (row < pos[0, n])
            m = m & ((col >= pos[1, n]) if b == 0 else (col < pos[1, n]))
            part = jnp.where(m, g[n, plane, q, cols], 0.0)
            acc = part if acc is None else acc + part
        return acc

    lo, hi = slice(0, H), slice(H, W)

    def outer(plane, _):
        for j in range(4):
            out_row[0, plane, :, j * H:(j + 1) * H] = total(plane, lo, 0, j // 2, (lo, hi)[j % 2]).astype(BF16)
            out_row[1, plane, :, j * H:(j + 1) * H] = total(plane, hi, 1, j // 2, (lo, hi)[j % 2]).astype(BF16)
        for i, q in enumerate((hi, lo)):
            rows = slice(i * H, (i + 1) * H)
            out_col[0, plane, rows] = total(plane, q, i, 0, lo).astype(BF16)
            out_col[1, plane, rows] = total(plane, q, i, 1, hi).astype(BF16)
        return 0

    def inner(plane, _):
        for i, q in enumerate((hi, lo)):
            rows = slice(i * H, (i + 1) * H)
            center[plane, rows, 0:H] = total(plane, q, i, 0, hi)
            center[plane, rows, H:] = total(plane, q, i, 1, lo)
        return 0

    def add_fold(s, k):
        dr, dc = AROUND[k]
        e = half_of(-dr)
        f = half_of(-dc)

        @pl.when(lands(k))
        def _():
            fold(s, k).wait_recv()
            for plane in (2 * s, 2 * s + 1):
                if dr:
                    got = got_row[0 if dr < 0 else 1, plane, :, spot_of(dc)]
                else:
                    got = got_col[0 if dc < 0 else 1, plane]
                center[plane, e, f] += got.astype(F32)

    lax.fori_loop(2, 4, outer, 0)
    fold_start(1)

    lax.fori_loop(2, 4, inner, 0)

    def e5(n, q, re, im):
        p, t = prop[0, q], prop[1, q]
        put(n, q, p * re + t * im, p * im - t * re)

    def e6(n, q, re, im):
        p, t = pr[n, 0, q], pr[n, 1, q]
        g[n, 0, q] = p * re + t * im
        g[n, 1, q] = p * im - t * re
        a, b = pick(n, 0, q), pick(n, 1, q)
        wave[n, 0, q] = a * re + b * im
        wave[n, 1, q] = a * im - b * re

    def probe_back(n):
        sums[0] += back(wave[n, 0], n)
        sums[1] += back(wave[n, 1], n)
    sweep(transform(v, fwd_t, inv_t, e5), transform(u, inv_t, fwd_t, e6), probe_back)

    mine = pl.ds(pl.multiple_of(core * H, H), H)
    other = pl.ds(pl.multiple_of((1 - core) * H, H), H)
    core_out[...] = sums[:, other].astype(BF16)
    swap = to_mate(core_out, core_got, 0, mates[0])
    swap.start()
    fold_turn(1)
    lax.fori_loop(0, 2, outer, 0)
    fold_start(0)

    Q = H // XS
    swap.wait()
    sums[:, mine] = sums[:, mine] + core_got[...].astype(F32)
    spread = []
    for d in range(1, XS):
        at = pl.multiple_of(core * H + lax.rem(xi + d, XS) * Q, Q)
        x_out[d - 1] = sums[:, pl.ds(at, Q)].astype(BF16)
        cp = to_mate(x_out.at[d - 1], x_got.at[d - 1], d, mates[1 + d])
        cp.start()
        spread.append(cp)
    fold_turn(0)
    acc = sums[:, pl.ds(pl.multiple_of(core * H + xi * Q, Q), Q)]
    for d in range(1, XS):
        spread[d - 1].wait()
        acc = acc + x_got[d - 1].astype(F32)
    z_out[...] = acc.astype(BF16)
    cross = to_mate(z_out, z_got, XS, mates[1])
    cross.start()
    lax.fori_loop(0, 2, inner, 0)
    for k in range(8):
        add_fold(1, k)
    cross.wait()
    tot = z_out[...].astype(F32) + z_got[...].astype(F32)
    scale = 1.0 / jnp.sqrt(tot[2] + 1e-06)
    here = pl.ds(pl.multiple_of(core * H + xi * Q, Q), Q)
    fin[0, here] = (tot[0] * scale).astype(BF16)
    fin[1, here] = (tot[1] * scale).astype(BF16)
    gather = []
    for d in range(1, XS):
        cp = to_mate(fin.at[:, here], fin.at[:, here], XS + d, mates[1 + d])
        cp.start()
        gather.append(cp)
    for d in range(1, XS):
        gather[d - 1].wait()
    last = to_mate(fin.at[:, mine], fin.at[:, mine], 2 * XS, mates[0])
    last.start()
    for k in (6, 7, 0, 1, 2, 3, 4, 5):
        add_fold(0, k)
    last.wait()
    for k in range(4):
        grad[k] = center[k].astype(BF16)
    for s in range(2):
        halo_sent(s)
        fold_sent(s)


def widen_kernel(grad, probe, wide_grad, wide_probe):
    for k in range(4):
        wide_grad[k] = grad[k].astype(F32)
    for k in range(2):
        wide_probe[k] = probe[k].astype(F32)


def tables():
    k = np.arange(W)
    ang = 2.0 * np.pi * ((k[:, None] * k[None, :]) % W) / W
    both = np.stack([np.cos(ang), np.sin(ang)]) / np.sqrt(W)
    return jnp.asarray(both.astype(np.float32)).astype(BF16)


def on_device(n_row, n_col, object_slices, probe_wave_parts, prop_phase, measured, positions):
    vm = pl.BlockSpec(memory_space=pltpu.VMEM)
    anys = pl.BlockSpec(memory_space=pl.ANY)
    shape = jax.ShapeDtypeStruct
    Q = H // XS
    dma = pltpu.SemaphoreType.DMA
    grad, probe_grad = pl.pallas_call(
        functools.partial(kernel, n_row, n_col),
        out_shape=(shape((4, W, W), BF16), shape((2, W, W), BF16)),
        in_specs=[pl.BlockSpec(memory_space=pltpu.SMEM), anys, vm, vm, anys, vm],
        out_specs=(vm, vm),
        scratch_shapes=[
            pltpu.VMEM((2 * W, 2 * W), BF16), pltpu.VMEM((2 * W, 2 * W), BF16), pltpu.VMEM((2, W, W), F32),
            pltpu.VMEM((NP, 2 * W, W), BF16), pltpu.VMEM((NP, 2 * W, W), BF16), pltpu.VMEM((NP, W, 2 * W), BF16),
            pltpu.VMEM((4, 2 * W, 2 * W), BF16), pltpu.VMEM((NP, 2, W, W), F32), pltpu.VMEM((NP, 2, W, W), F32),
            pltpu.VMEM((NP, 4, W, W), F32), pltpu.VMEM((3, W, W), F32), pltpu.VMEM((NP, W, W), F32),
            pltpu.VMEM((2, 4, H, 2 * W), BF16), pltpu.VMEM((2, 4, W, H), BF16),
            pltpu.VMEM((2, 4, H, 2 * W), BF16), pltpu.VMEM((2, 4, W, H), BF16),
            pltpu.VMEM((3, H, W), BF16), pltpu.VMEM((3, H, W), BF16),
            pltpu.VMEM((XS - 1, 3, Q, W), BF16), pltpu.VMEM((XS - 1, 3, Q, W), BF16),
            pltpu.VMEM((3, Q, W), BF16), pltpu.VMEM((3, Q, W), BF16), pltpu.VMEM((4, W, W), F32),
            pltpu.VMEM((2, 4, 2, H, H), BF16), dma((2,)), dma((2, 4)), dma((2, 4)), dma((2, 8)), dma((2, 8)), dma((2, 8)), dma((2, 8)), dma((2 * XS + 1,)), dma((2 * XS + 1,)),
        ],
        compiler_params=pltpu.CompilerParams(collective_id=0, has_side_effects=True, vmem_limit_bytes=60 << 20),
    )(positions.T, object_slices.reshape(4, W, W), probe_wave_parts[0], prop_phase, measured, tables())
    wide_grad, wide_probe = pl.pallas_call(
        widen_kernel,
        out_shape=(shape((4, W, W), F32), shape((2, W, W), F32)),
        in_specs=[vm, vm],
        out_specs=(vm, vm),
    )(grad, probe_grad)
    return wide_grad.reshape(2, 2, W, W), wide_probe[None]


def solution(mesh):
    return jax.shard_map(
        functools.partial(on_device, mesh.shape["row"], mesh.shape["col"]),
        mesh=mesh,
        in_specs=(
            P(None, None, "row", "col"),
            P("col", None, None, None),
            P(),
            P(("row", "col"), None, None),
            P(("row", "col"), None),
        ),
        out_specs=(P(None, None, "row", "col"), P("col", None, None, None)),
        check_vma=False,
    )
```

```python
import functools

import jax
import jax.numpy as jnp
import numpy as np
from jax import lax
from jax.experimental import pallas as pl
from jax.experimental.pallas import tpu as pltpu
from jax.sharding import PartitionSpec as P

W = 256
H = 128
NP = 4
RC = 128
UNROLL = 4
F32, BF16 = jnp.float32, jnp.bfloat16
MESH = pl.DeviceIdType.MESH
AROUND = ((-1, 0), (1, 0), (-1, -1), (-1, 1), (1, -1), (1, 1), (0, -1), (0, 1))
CHUNKS = [slice(i, i + RC) for i in range(0, W, RC)]
XS, ZS = 4, 2
LOOP = 8
TURNS = [(dr, dc) for dc in (-1, 1) for dr in (-1, 1)]


def half_of(step):
    return {-1: slice(0, H), 0: slice(0, W), 1: slice(H, W)}[step]


def rim_of(step):
    return {-1: slice(3 * H, 4 * H), 0: slice(H, 3 * H), 1: slice(0, H)}[step]


def spot_of(step):
    return {-1: slice(0, H), 0: slice(H, 3 * H), 1: slice(3 * H, 4 * H)}[step]


def moved(q, by):
    return slice(q.start + by, q.stop + by)


def kernel(
    n_row, n_col,
    pos, obj, probe_in, phase_in, meas_in, cs_in,
    center, fin,
    probe, phase, cs, fwd_t, inv_t, prop, u, v, h, ext, pr, wave, g, sums, meas,
    out_row, out_col, got_row, got_col,
    core_out, core_got, x_out, x_got, z_out, z_got,
    turned, local_sem, turn_send, turn_recv, halo_send, halo_recv, fold_send, fold_recv, sum_send, sum_recv,
):
    r, c = lax.axis_index("row"), lax.axis_index("col")
    core = lax.rem(r, 2)
    xi = lax.rem(r // 2, XS)
    zi = r // (2 * XS)

    def inside(dr, dc):
        ok = None
        for idx, step, count in ((r, dr, n_row), (c, dc, n_col)):
            if step:
                here = (idx > 0) if step < 0 else (idx < count - 1)
                ok = here if ok is None else ok & here
        return ok

    def col_far(at, step):
        return lax.rem(at, LOOP) == (LOOP - 1 if step > 0 else 0)

    def row_far(at, step):
        return at == (n_row // ZS - 1 if step > 0 else n_row // ZS)

    def bent(row, col, dr, dc):
        return col_far(col, dc) & jnp.logical_not(row_far(row, dr))

    def leaves(k):
        dr, dc = AROUND[k]
        ok = inside(dr, dc)
        return ok & jnp.logical_not(bent(r, c, dr, dc)) if dr and dc else ok

    def lands(k):
        dr, dc = AROUND[k]
        ok = inside(-dr, -dc)
        return ok & jnp.logical_not(bent(r - dr, c - dc, dr, dc)) if dr and dc else ok

    def row_at(z, x, k):
        return (z * XS + x) * 2 + k

    mates = [(row_at(zi, xi, 1 - core), c), (row_at(1 - zi, xi, core), c)]
    mates += [(row_at(zi, lax.rem(xi + d, XS), core), c) for d in range(1, XS)]

    crossed = [(row_at(zi, lax.rem(xi + d, XS), 1 - core), c) for d in range(1, XS)]

    barrier = pltpu.get_barrier_semaphore()
    for dr, dc in AROUND:
        @pl.when(inside(dr, dc))
        def _():
            pl.semaphore_signal(barrier, inc=1, device_id=(r + dr, c + dc), device_id_type=MESH)
    for mate in mates[1:] + crossed:
        pl.semaphore_signal(barrier, inc=1, device_id=mate, device_id_type=MESH)
    own = pltpu.make_async_copy(obj, ext.at[:, pl.ds(H, W), pl.ds(H, W)], local_sem.at[0])
    own.start()
    load = pltpu.make_async_copy(meas_in, meas, local_sem.at[1])
    load.start()
    small = [
        pltpu.make_async_copy(a, b, local_sem.at[2 + i])
        for i, (a, b) in enumerate(((probe_in, probe), (phase_in, phase), (cs_in, cs)))
    ]
    for cp in small:
        cp.start()
    peers = jnp.int32(len(mates) - 1 + len(crossed))
    for dr, dc in AROUND:
        peers = peers + inside(dr, dc).astype(jnp.int32)
    pl.semaphore_wait(barrier, peers)

    def halo(s, k):
        dr, dc = AROUND[k]
        a, b, e, f = half_of(dr), half_of(dc), rim_of(dr), rim_of(dc)
        return pltpu.make_async_remote_copy(
            src_ref=obj.at[pl.ds(2 * s, 2), a, b],
            dst_ref=ext.at[pl.ds(2 * s, 2), e, f],
            send_sem=halo_send.at[s, k],
            recv_sem=halo_recv.at[s, k],
            device_id=(r + dr, c + dc),
            device_id_type=MESH,
        )

    def fold(s, k):
        dr, dc = AROUND[k]
        if dr:
            i = 0 if dr < 0 else 1
            place = (i, pl.ds(2 * s, 2), slice(None), spot_of(dc))
            src, dst = out_row.at[place], got_row.at[place]
        else:
            i = 0 if dc < 0 else 1
            place = (i, pl.ds(2 * s, 2))
            src, dst = out_col.at[place], got_col.at[place]
        return pltpu.make_async_remote_copy(
            src_ref=src, dst_ref=dst, send_sem=fold_send.at[s, k], recv_sem=fold_recv.at[s, k],
            device_id=(r + dr, c + dc), device_id_type=MESH,
        )

    def to_mate(src, dst, i, mate):
        return pltpu.make_async_remote_copy(
            src_ref=src, dst_ref=dst, send_sem=sum_send.at[i], recv_sem=sum_recv.at[i],
            device_id=mate, device_id_type=MESH,
        )

    def pass_on(s, t):
        dr, dc = TURNS[t]
        e, f = half_of(dr), rim_of(dc)
        return pltpu.make_async_remote_copy(
            src_ref=ext.at[pl.ds(2 * s, 2), moved(e, H), f],
            dst_ref=ext.at[pl.ds(2 * s, 2), rim_of(dr), f],
            send_sem=turn_send.at[s, t],
            recv_sem=halo_recv.at[s, AROUND.index((dr, dc))],
            device_id=(r + dr, c),
            device_id_type=MESH,
        )

    def turn(s, t):
        dr, dc = TURNS[t]
        k = AROUND.index((dr, dc))
        place = (0 if dr < 0 else 1, pl.ds(2 * s, 2), slice(None), spot_of(dc))
        return pltpu.make_async_remote_copy(
            src_ref=out_row.at[place], dst_ref=turned.at[s, t], send_sem=fold_send.at[s, k], recv_sem=turn_recv.at[s, t],
            device_id=(r + dr, c), device_id_type=MESH,
        )

    def passes(t):
        dr, dc = TURNS[t]
        return inside(0, -dc) & inside(dr, 0) & bent(r, c - dc, dr, dc)

    def gets(t):
        dr, dc = TURNS[t]
        return inside(0, dc) & inside(-dr, 0) & bent(r - dr, c, dr, dc)

    def halo_start(s):
        for k in range(8):
            @pl.when(leaves(k))
            def _():
                halo(s, k).start()

    def halo_turn(s):
        for dc in (-1, 1):
            @pl.when(inside(0, -dc) & col_far(c - dc, dc))
            def _():
                halo(s, AROUND.index((0, dc))).wait_recv()
        for t in range(4):
            @pl.when(passes(t))
            def _():
                pass_on(s, t).start()

    def halo_arrived(s):
        for k, (dr, dc) in enumerate(AROUND):
            ok = inside(-dr, -dc)
            if not dr:
                ok = ok & jnp.logical_not(col_far(c - dc, dc))

            @pl.when(ok)
            def _():
                halo(s, k).wait_recv()

    def halo_sent(s):
        for k in range(8):
            @pl.when(leaves(k))
            def _():
                halo(s, k).wait_send()
        for t in range(4):
            @pl.when(passes(t))
            def _():
                pass_on(s, t).wait_send()

    def fold_start(s):
        for k, (dr, dc) in enumerate(AROUND):
            ok = leaves(k)
            if not dr:
                ok = ok & jnp.logical_not(col_far(c, dc))
            elif dc:
                @pl.when(inside(dr, dc) & bent(r, c, dr, dc))
                def _():
                    turn(s, TURNS.index((dr, dc))).start()

            @pl.when(ok)
            def _():
                fold(s, k).start()

    def fold_turn(s):
        for t, (dr, dc) in enumerate(TURNS):
            @pl.when(gets(t))
            def _():
                turn(s, t).wait_recv()
                rows = half_of(-dr)
                for p in range(2):
                    i = (0 if dc < 0 else 1, 2 * s + p, rows)
                    out_col[i] = (out_col[i].astype(F32) + turned[s, t, p].astype(F32)).astype(BF16)
        for dc in (-1, 1):
            @pl.when(inside(0, dc) & col_far(c, dc))
            def _():
                fold(s, AROUND.index((0, dc))).start()

    def fold_sent(s):
        for k, (dr, dc) in enumerate(AROUND):
            @pl.when(inside(dr, dc))
            def _():
                fold(s, k).wait_send()

    halo_start(0)
    halo_start(1)

    for dr, dc in AROUND:
        @pl.when(jnp.logical_not(inside(-dr, -dc)))
        def _():
            e, f = rim_of(dr), rim_of(dc)
            ext[:, e, f] = jnp.zeros((4, e.stop - e.start, f.stop - f.start), BF16)

    for cp in small:
        cp.wait()
    cos_t, sin_t = cs[0], cs[1]
    for t, sgn in ((fwd_t, 1), (inv_t, -1)):
        t[0:W, 0:W] = cos_t
        t[W:, W:] = cos_t
        t[0:W, W:] = sin_t if sgn > 0 else -sin_t
        t[W:, 0:W] = -sin_t if sgn > 0 else sin_t
    for q in CHUNKS:
        prop[0, q] = jnp.cos(phase[q])
        prop[1, q] = jnp.sin(phase[q])
    sums[...] = jnp.zeros_like(sums)

    def rolled(n, _):
        for k in range(2):
            pr[n, k] = pltpu.roll(pltpu.roll(probe[k], pos[0, n], 0), pos[1, n], 1)
        return 0
    lax.fori_loop(0, NP, rolled, 0)

    def transform(src, lt, rt, epilogue):
        def run(n):
            half = jnp.dot(lt[...], src[n], preferred_element_type=F32)
            h[n, :, 0:W] = half[0:W].astype(BF16)
            h[n, :, W:] = half[W:].astype(BF16)
            for q in CHUNKS:
                o = jnp.dot(h[n, q, :], rt[...], preferred_element_type=F32)
                epilogue(n, q, o[:, 0:W], o[:, W:])
        return run

    def put(n, q, re, im):
        u[n, q, :] = re.astype(BF16)
        u[n, moved(q, W), :] = im.astype(BF16)

    def pick(n, plane, q):
        col = lax.broadcasted_iota(jnp.int32, (RC, W), 1) >= pos[1, n]
        row = lax.broadcasted_iota(jnp.int32, (RC, W), 0) + q.start >= pos[0, n]
        q2 = moved(q, W)
        a = jnp.where(col, ext[plane, q, 0:W].astype(F32), ext[plane, q, W:].astype(F32))
        b = jnp.where(col, ext[plane, q2, 0:W].astype(F32), ext[plane, q2, W:].astype(F32))
        return jnp.where(row, a, b)

    def sweep(*stages):
        def some(i, _):
            for stage in stages:
                for k in range(UNROLL):
                    stage(i * UNROLL + k)
            return 0
        if UNROLL == NP:
            some(0, 0)
        else:
            lax.fori_loop(0, NP // UNROLL, some, 0)

    def back(x, n):
        return pltpu.roll(pltpu.roll(x, W - pos[0, n], 0), W - pos[1, n], 1)

    halo_turn(0)
    own.wait()
    halo_arrived(0)

    def first_exit(n):
        for q in CHUNKS:
            a, b = pick(n, 0, q), pick(n, 1, q)
            p, t = pr[n, 0, q], pr[n, 1, q]
            put(n, q, p * a - t * b, p * b + t * a)
            g[n, 0, q] = a * a + b * b

    def bright(n):
        sums[2] += back(g[n, 0], n)

    def e1(n, q, re, im):
        p, t = prop[0, q], prop[1, q]
        put(n, q, p * re - t * im, p * im + t * re)

    def e2(n, q, re, im):
        wave[n, 0, q] = re
        wave[n, 1, q] = im
    sweep(first_exit, bright, transform(u, fwd_t, inv_t, e1))
    halo_turn(1)
    sweep(transform(u, inv_t, fwd_t, e2))

    load.wait()
    halo_arrived(1)

    def second_exit(n):
        for q in CHUNKS:
            a, b = pick(n, 2, q), pick(n, 3, q)
            re, im = wave[n, 0, q], wave[n, 1, q]
            put(n, q, re * a - im * b, re * b + im * a)

    def e3(n, q, re, im):
        res = re * re + im * im - meas[n, q]
        put(n, q, res * re, res * im)

    def e4(n, q, re, im):
        wr, wi = wave[n, 0, q], wave[n, 1, q]
        g[n, 2, q] = wr * re + wi * im
        g[n, 3, q] = wr * im - wi * re
        a, b = pick(n, 2, q), pick(n, 3, q)
        v[n, q] = (a * re + b * im).astype(BF16)
        v[n, moved(q, W)] = (a * im - b * re).astype(BF16)
    sweep(second_exit, transform(u, fwd_t, inv_t, e3), transform(u, inv_t, fwd_t, e4))

    def total(plane, q, a, b, cols):
        acc = None
        for n in range(NP):
            row = lax.broadcasted_iota(jnp.int32, (q.stop - q.start, H), 0) + q.start
            col = lax.broadcasted_iota(jnp.int32, (q.stop - q.start, H), 1) + cols.start
            m = (row >= pos[0, n]) if a == 0 else (row < pos[0, n])
            m = m & ((col >= pos[1, n]) if b == 0 else (col < pos[1, n]))
            part = jnp.where(m, g[n, plane, q, cols], 0.0)
            acc = part if acc is None else acc + part
        return acc

    lo, hi = slice(0, H), slice(H, W)

    def outer(plane, _):
        for j in range(4):
            out_row[0, plane, :, j * H:(j + 1) * H] = total(plane, lo, 0, j // 2, (lo, hi)[j % 2]).astype(BF16)
            out_row[1, plane, :, j * H:(j + 1) * H] = total(plane, hi, 1, j // 2, (lo, hi)[j % 2]).astype(BF16)
        for i, q in enumerate((hi, lo)):
            rows = slice(i * H, (i + 1) * H)
            out_col[0, plane, rows] = total(plane, q, i, 0, lo).astype(BF16)
            out_col[1, plane, rows] = total(plane, q, i, 1, hi).astype(BF16)
        return 0

    def inner(plane, _):
        for i, q in enumerate((hi, lo)):
            rows = slice(i * H, (i + 1) * H)
            center[plane, rows, 0:H] = total(plane, q, i, 0, hi)
            center[plane, rows, H:] = total(plane, q, i, 1, lo)
        return 0

    def add_fold(s, k):
        dr, dc = AROUND[k]
        e = half_of(-dr)
        f = half_of(-dc)

        @pl.when(lands(k))
        def _():
            fold(s, k).wait_recv()
            for plane in (2 * s, 2 * s + 1):
                if dr:
                    got = got_row[0 if dr < 0 else 1, plane, :, spot_of(dc)]
                else:
                    got = got_col[0 if dc < 0 else 1, plane]
                center[plane, e, f] += got.astype(F32)

    lax.fori_loop(2, 4, outer, 0)
    fold_start(1)

    lax.fori_loop(2, 4, inner, 0)

    def e5(n, q, re, im):
        p, t = prop[0, q], prop[1, q]
        put(n, q, p * re + t * im, p * im - t * re)

    def e6(n, q, re, im):
        p, t = pr[n, 0, q], pr[n, 1, q]
        g[n, 0, q] = p * re + t * im
        g[n, 1, q] = p * im - t * re
        a, b = pick(n, 0, q), pick(n, 1, q)
        wave[n, 0, q] = a * re + b * im
        wave[n, 1, q] = a * im - b * re

    def probe_back(n):
        sums[0] += back(wave[n, 0], n)
        sums[1] += back(wave[n, 1], n)
    sweep(transform(v, fwd_t, inv_t, e5), transform(u, inv_t, fwd_t, e6), probe_back)

    mine = pl.ds(pl.multiple_of(core * H, H), H)
    other = pl.ds(pl.multiple_of((1 - core) * H, H), H)
    core_out[...] = sums[:, other].astype(BF16)
    swap = to_mate(core_out, core_got, 0, mates[0])
    swap.start()
    fold_turn(1)
    lax.fori_loop(0, 2, outer, 0)
    fold_start(0)

    Q = H // XS
    swap.wait()
    sums[:, mine] = sums[:, mine] + core_got[...].astype(F32)
    spread = []
    for d in range(1, XS):
        at = pl.multiple_of(core * H + lax.rem(xi + d, XS) * Q, Q)
        x_out[d - 1] = sums[:, pl.ds(at, Q)].astype(BF16)
        cp = to_mate(x_out.at[d - 1], x_got.at[d - 1], d, mates[1 + d])
        cp.start()
        spread.append(cp)
    lax.fori_loop(0, 2, inner, 0)
    acc = sums[:, pl.ds(pl.multiple_of(core * H + xi * Q, Q), Q)]
    for d in range(1, XS):
        spread[d - 1].wait()
        acc = acc + x_got[d - 1].astype(F32)
    z_out[...] = acc.astype(BF16)
    cross = to_mate(z_out, z_got, XS, mates[1])
    cross.start()
    fold_turn(0)
    for k in range(8):
        add_fold(1, k)
    cross.wait()
    tot = z_out[...].astype(F32) + z_got[...].astype(F32)
    scale = 1.0 / jnp.sqrt(tot[2] + 1e-06)
    here = pl.ds(pl.multiple_of(core * H + xi * Q, Q), Q)
    fin[0, here] = (tot[0] * scale).astype(BF16)
    fin[1, here] = (tot[1] * scale).astype(BF16)
    gather = []
    for i, mate in enumerate(mates[2:] + crossed + mates[:1]):
        cp = to_mate(fin.at[:, here], fin.at[:, here], XS + 1 + i, mate)
        cp.start()
        gather.append(cp)
    for k in (6, 7, 0, 1, 2, 3, 4, 5):
        add_fold(0, k)
    for cp in gather:
        cp.wait()
    for s in range(2):
        halo_sent(s)
        fold_sent(s)


def finish_kernel(grad, probe, grad_out, probe_out, sem):
    put = pltpu.make_async_copy(grad, grad_out, sem)
    put.start()
    for k in range(2):
        probe_out[k] = probe[k].astype(F32)
    put.wait()


def tables():
    k = np.arange(W)
    ang = 2.0 * np.pi * ((k[:, None] * k[None, :]) % W) / W
    both = np.stack([np.cos(ang), np.sin(ang)]) / np.sqrt(W)
    return jnp.asarray(both.astype(np.float32)).astype(BF16)


def on_device(n_row, n_col, object_slices, probe_wave_parts, prop_phase, measured, positions):
    vm = pl.BlockSpec(memory_space=pltpu.VMEM)
    anys = pl.BlockSpec(memory_space=pl.ANY)
    shape = jax.ShapeDtypeStruct
    Q = H // XS
    dma = pltpu.SemaphoreType.DMA
    grad, probe_grad = pl.pallas_call(
        functools.partial(kernel, n_row, n_col),
        out_shape=(pltpu.VMEM((4, W, W), F32), pltpu.VMEM((2, W, W), BF16)),
        in_specs=[pl.BlockSpec(memory_space=pltpu.SMEM)] + [anys] * 5,
        out_specs=(vm, vm),
        scratch_shapes=[
            pltpu.VMEM((2, W, W), F32), pltpu.VMEM((W, W), F32), pltpu.VMEM((2, W, W), BF16),
            pltpu.VMEM((2 * W, 2 * W), BF16), pltpu.VMEM((2 * W, 2 * W), BF16), pltpu.VMEM((2, W, W), F32),
            pltpu.VMEM((NP, 2 * W, W), BF16), pltpu.VMEM((NP, 2 * W, W), BF16), pltpu.VMEM((NP, W, 2 * W), BF16),
            pltpu.VMEM((4, 2 * W, 2 * W), BF16), pltpu.VMEM((NP, 2, W, W), F32), pltpu.VMEM((NP, 2, W, W), F32),
            pltpu.VMEM((NP, 4, W, W), F32), pltpu.VMEM((3, W, W), F32), pltpu.VMEM((NP, W, W), F32),
            pltpu.VMEM((2, 4, H, 2 * W), BF16), pltpu.VMEM((2, 4, W, H), BF16),
            pltpu.VMEM((2, 4, H, 2 * W), BF16), pltpu.VMEM((2, 4, W, H), BF16),
            pltpu.VMEM((3, H, W), BF16), pltpu.VMEM((3, H, W), BF16),
            pltpu.VMEM((XS - 1, 3, Q, W), BF16), pltpu.VMEM((XS - 1, 3, Q, W), BF16),
            pltpu.VMEM((3, Q, W), BF16), pltpu.VMEM((3, Q, W), BF16),
            pltpu.VMEM((2, 4, 2, H, H), BF16), dma((5,)), dma((2, 4)), dma((2, 4)), dma((2, 8)), dma((2, 8)), dma((2, 8)), dma((2, 8)), dma((3 * XS,)), dma((3 * XS,)),
        ],
        compiler_params=pltpu.CompilerParams(collective_id=0, has_side_effects=True, vmem_limit_bytes=60 << 20),
    )(positions.T, object_slices.reshape(4, W, W), probe_wave_parts[0], prop_phase, measured, tables())
    grad_out, probe_out = pl.pallas_call(
        finish_kernel,
        out_shape=(shape((4, W, W), F32), shape((2, W, W), F32)),
        in_specs=[vm, vm],
        out_specs=(anys, vm),
        scratch_shapes=[dma],
    )(pltpu.with_memory_space_constraint(grad, pltpu.VMEM), pltpu.with_memory_space_constraint(probe_grad, pltpu.VMEM))
    return grad_out.reshape(2, 2, W, W), probe_out[None]


def solution(mesh):
    return jax.shard_map(
        functools.partial(on_device, mesh.shape["row"], mesh.shape["col"]),
        mesh=mesh,
        in_specs=(
            P(None, None, "row", "col"),
            P("col", None, None, None),
            P(),
            P(("row", "col"), None, None),
            P(("row", "col"), None),
        ),
        out_specs=(P(None, None, "row", "col"), P("col", None, None, None)),
        check_vma=False,
    )
```

```python
import functools

import jax
import jax.numpy as jnp
import numpy as np
from jax import lax
from jax.experimental import pallas as pl
from jax.experimental.pallas import tpu as pltpu
from jax.sharding import PartitionSpec as P

W = 256
H = 128
NP = 4
RC = 128
UNROLL = 4
F32, BF16 = jnp.float32, jnp.bfloat16
MESH = pl.DeviceIdType.MESH
AROUND = ((-1, 0), (1, 0), (-1, -1), (-1, 1), (1, -1), (1, 1), (0, -1), (0, 1))
CHUNKS = [slice(i, i + RC) for i in range(0, W, RC)]
PARTS = [slice(0, H), slice(H, W)]
XS, ZS = 4, 2
LOOP = 8
TURNS = [(dr, dc) for dc in (-1, 1) for dr in (-1, 1)]


def half_of(step):
    return {-1: slice(0, H), 0: slice(0, W), 1: slice(H, W)}[step]


def rim_of(step):
    return {-1: slice(3 * H, 4 * H), 0: slice(H, 3 * H), 1: slice(0, H)}[step]


def spot_of(step):
    return {-1: slice(0, H), 0: slice(H, 3 * H), 1: slice(3 * H, 4 * H)}[step]


def moved(q, by):
    return slice(q.start + by, q.stop + by)


def kernel(
    n_row, n_col,
    pos, obj, probe_in, phase_in, meas_in, cs_in,
    center, fin,
    probe, phase, cs, fwd_t, inv_t, prop, u, v, h, ext, pr, wave, g, sums, meas,
    out_row, out_col, got_row, got_col,
    core_out, core_got, x_out, x_got, z_out, z_got,
    turned, local_sem, turn_send, turn_recv, halo_send, halo_recv, fold_send, fold_recv, sum_send, sum_recv,
):
    r, c = lax.axis_index("row"), lax.axis_index("col")
    core = lax.rem(r, 2)
    xi = lax.rem(r // 2, XS)
    zi = r // (2 * XS)

    def inside(dr, dc):
        ok = None
        for idx, step, count in ((r, dr, n_row), (c, dc, n_col)):
            if step:
                here = (idx > 0) if step < 0 else (idx < count - 1)
                ok = here if ok is None else ok & here
        return ok

    def col_far(at, step):
        return lax.rem(at, LOOP) == (LOOP - 1 if step > 0 else 0)

    def row_far(at, step):
        return at == (n_row // ZS - 1 if step > 0 else n_row // ZS)

    def bent(row, col, dr, dc):
        return col_far(col, dc) & jnp.logical_not(row_far(row, dr))

    def leaves(k):
        dr, dc = AROUND[k]
        ok = inside(dr, dc)
        return ok & jnp.logical_not(bent(r, c, dr, dc)) if dr and dc else ok

    def lands(k):
        dr, dc = AROUND[k]
        ok = inside(-dr, -dc)
        return ok & jnp.logical_not(bent(r - dr, c - dc, dr, dc)) if dr and dc else ok

    def row_at(z, x, k):
        return (z * XS + x) * 2 + k

    mates = [(row_at(zi, xi, 1 - core), c), (row_at(1 - zi, xi, core), c)]
    mates += [(row_at(zi, lax.rem(xi + d, XS), core), c) for d in range(1, XS)]

    crossed = [(row_at(zi, lax.rem(xi + d, XS), 1 - core), c) for d in range(1, XS)]

    barrier = pltpu.get_barrier_semaphore()
    for dr, dc in AROUND:
        @pl.when(inside(dr, dc))
        def _():
            pl.semaphore_signal(barrier, inc=1, device_id=(r + dr, c + dc), device_id_type=MESH)
    for mate in mates[1:] + crossed:
        pl.semaphore_signal(barrier, inc=1, device_id=mate, device_id_type=MESH)
    own = pltpu.make_async_copy(obj, ext.at[:, pl.ds(H, W), pl.ds(H, W)], local_sem.at[0])
    own.start()
    load = pltpu.make_async_copy(meas_in, meas, local_sem.at[1])
    load.start()
    small = [
        pltpu.make_async_copy(a, b, local_sem.at[2 + i])
        for i, (a, b) in enumerate(((probe_in, probe), (phase_in, phase), (cs_in, cs)))
    ]
    for cp in small:
        cp.start()
    peers = jnp.int32(len(mates) - 1 + len(crossed))
    for dr, dc in AROUND:
        peers = peers + inside(dr, dc).astype(jnp.int32)
    pl.semaphore_wait(barrier, peers)

    def halo(s, k):
        dr, dc = AROUND[k]
        a, b, e, f = half_of(dr), half_of(dc), rim_of(dr), rim_of(dc)
        return pltpu.make_async_remote_copy(
            src_ref=obj.at[pl.ds(2 * s, 2), a, b],
            dst_ref=ext.at[pl.ds(2 * s, 2), e, f],
            send_sem=halo_send.at[s, k],
            recv_sem=halo_recv.at[s, k],
            device_id=(r + dr, c + dc),
            device_id_type=MESH,
        )

    def fold(s, k):
        dr, dc = AROUND[k]
        if dr:
            i = 0 if dr < 0 else 1
            place = (i, pl.ds(2 * s, 2), slice(None), spot_of(dc))
            src, dst = out_row.at[place], got_row.at[place]
        else:
            i = 0 if dc < 0 else 1
            place = (i, pl.ds(2 * s, 2))
            src, dst = out_col.at[place], got_col.at[place]
        return pltpu.make_async_remote_copy(
            src_ref=src, dst_ref=dst, send_sem=fold_send.at[s, k], recv_sem=fold_recv.at[s, k],
            device_id=(r + dr, c + dc), device_id_type=MESH,
        )

    def to_mate(src, dst, i, mate):
        return pltpu.make_async_remote_copy(
            src_ref=src, dst_ref=dst, send_sem=sum_send.at[i], recv_sem=sum_recv.at[i],
            device_id=mate, device_id_type=MESH,
        )

    def pass_on(s, t):
        dr, dc = TURNS[t]
        e, f = half_of(dr), rim_of(dc)
        return pltpu.make_async_remote_copy(
            src_ref=ext.at[pl.ds(2 * s, 2), moved(e, H), f],
            dst_ref=ext.at[pl.ds(2 * s, 2), rim_of(dr), f],
            send_sem=turn_send.at[s, t],
            recv_sem=halo_recv.at[s, AROUND.index((dr, dc))],
            device_id=(r + dr, c),
            device_id_type=MESH,
        )

    def turn(s, t):
        dr, dc = TURNS[t]
        k = AROUND.index((dr, dc))
        place = (0 if dr < 0 else 1, pl.ds(2 * s, 2), slice(None), spot_of(dc))
        return pltpu.make_async_remote_copy(
            src_ref=out_row.at[place], dst_ref=turned.at[s, t], send_sem=fold_send.at[s, k], recv_sem=turn_recv.at[s, t],
            device_id=(r + dr, c), device_id_type=MESH,
        )

    def passes(t):
        dr, dc = TURNS[t]
        return inside(0, -dc) & inside(dr, 0) & bent(r, c - dc, dr, dc)

    def gets(t):
        dr, dc = TURNS[t]
        return inside(0, dc) & inside(-dr, 0) & bent(r - dr, c, dr, dc)

    def halo_start(s):
        for k in range(8):
            @pl.when(leaves(k))
            def _():
                halo(s, k).start()

    def halo_turn(s):
        for dc in (-1, 1):
            @pl.when(inside(0, -dc) & col_far(c - dc, dc))
            def _():
                halo(s, AROUND.index((0, dc))).wait_recv()
        for t in range(4):
            @pl.when(passes(t))
            def _():
                pass_on(s, t).start()

    def halo_arrived(s):
        for k, (dr, dc) in enumerate(AROUND):
            ok = inside(-dr, -dc)
            if not dr:
                ok = ok & jnp.logical_not(col_far(c - dc, dc))

            @pl.when(ok)
            def _():
                halo(s, k).wait_recv()

    def halo_sent(s):
        for k in range(8):
            @pl.when(leaves(k))
            def _():
                halo(s, k).wait_send()
        for t in range(4):
            @pl.when(passes(t))
            def _():
                pass_on(s, t).wait_send()

    def fold_start(s):
        for k, (dr, dc) in enumerate(AROUND):
            ok = leaves(k)
            if not dr:
                ok = ok & jnp.logical_not(col_far(c, dc))
            elif dc:
                @pl.when(inside(dr, dc) & bent(r, c, dr, dc))
                def _():
                    turn(s, TURNS.index((dr, dc))).start()

            @pl.when(ok)
            def _():
                fold(s, k).start()

    def fold_turn(s):
        for t, (dr, dc) in enumerate(TURNS):
            @pl.when(gets(t))
            def _():
                turn(s, t).wait_recv()
                rows = half_of(-dr)
                for p in range(2):
                    i = (0 if dc < 0 else 1, 2 * s + p, rows)
                    out_col[i] = (out_col[i].astype(F32) + turned[s, t, p].astype(F32)).astype(BF16)
        for dc in (-1, 1):
            @pl.when(inside(0, dc) & col_far(c, dc))
            def _():
                fold(s, AROUND.index((0, dc))).start()

    def fold_sent(s):
        for k, (dr, dc) in enumerate(AROUND):
            @pl.when(inside(dr, dc))
            def _():
                fold(s, k).wait_send()

    halo_start(0)
    halo_start(1)

    for dr, dc in AROUND:
        @pl.when(jnp.logical_not(inside(-dr, -dc)))
        def _():
            e, f = rim_of(dr), rim_of(dc)
            ext[:, e, f] = jnp.zeros((4, e.stop - e.start, f.stop - f.start), BF16)

    for cp in small:
        cp.wait()
    cos_t, sin_t = cs[0], cs[1]
    for t, sgn in ((fwd_t, 1), (inv_t, -1)):
        t[0:W, 0:W] = cos_t
        t[W:, W:] = cos_t
        t[0:W, W:] = sin_t if sgn > 0 else -sin_t
        t[W:, 0:W] = -sin_t if sgn > 0 else sin_t
    for q in CHUNKS:
        prop[0, q] = jnp.cos(phase[q])
        prop[1, q] = jnp.sin(phase[q])
    sums[...] = jnp.zeros_like(sums)

    def rolled(n, _):
        for k in range(2):
            pr[n, k] = pltpu.roll(pltpu.roll(probe[k], pos[0, n], 0), pos[1, n], 1)
        return 0
    lax.fori_loop(0, NP, rolled, 0)

    def transform(src, lt, rt, epilogue):
        def run(n):
            half = jnp.dot(lt[...], src[n], preferred_element_type=F32)
            h[n, :, 0:W] = half[0:W].astype(BF16)
            h[n, :, W:] = half[W:].astype(BF16)
            for q in CHUNKS:
                o = jnp.dot(h[n, q, :], rt[...], preferred_element_type=F32)
                epilogue(n, q, o[:, 0:W], o[:, W:])
        return run

    def put(n, q, re, im):
        u[n, q, :] = re.astype(BF16)
        u[n, moved(q, W), :] = im.astype(BF16)

    def pick(n, plane, q):
        col = lax.broadcasted_iota(jnp.int32, (RC, W), 1) >= pos[1, n]
        row = lax.broadcasted_iota(jnp.int32, (RC, W), 0) + q.start >= pos[0, n]
        q2 = moved(q, W)
        a = jnp.where(col, ext[plane, q, 0:W].astype(F32), ext[plane, q, W:].astype(F32))
        b = jnp.where(col, ext[plane, q2, 0:W].astype(F32), ext[plane, q2, W:].astype(F32))
        return jnp.where(row, a, b)

    def sweep(*stages):
        def some(i, _):
            for stage in stages:
                for k in range(UNROLL):
                    stage(i * UNROLL + k)
            return 0
        if UNROLL == NP:
            some(0, 0)
        else:
            lax.fori_loop(0, NP // UNROLL, some, 0)

    def back(x, n):
        return pltpu.roll(pltpu.roll(x, W - pos[0, n], 0), W - pos[1, n], 1)

    halo_turn(0)
    own.wait()
    halo_arrived(0)

    def first_exit(n):
        for q in CHUNKS:
            a, b = pick(n, 0, q), pick(n, 1, q)
            p, t = pr[n, 0, q], pr[n, 1, q]
            put(n, q, p * a - t * b, p * b + t * a)
            g[n, 0, q] = a * a + b * b

    def bright(n):
        sums[2] += back(g[n, 0], n)

    def e1(n, q, re, im):
        p, t = prop[0, q], prop[1, q]
        put(n, q, p * re - t * im, p * im + t * re)

    def e2(n, q, re, im):
        wave[n, 0, q] = re
        wave[n, 1, q] = im
    into_spectrum = transform(u, fwd_t, inv_t, e1)

    def spectrum(n):
        into_spectrum(n)
        bright(n)
    sweep(first_exit, spectrum)
    halo_turn(1)
    sweep(transform(u, inv_t, fwd_t, e2))

    load.wait()
    halo_arrived(1)

    def second_exit(n):
        for q in CHUNKS:
            a, b = pick(n, 2, q), pick(n, 3, q)
            re, im = wave[n, 0, q], wave[n, 1, q]
            put(n, q, re * a - im * b, re * b + im * a)

    def e3(n, q, re, im):
        res = re * re + im * im - meas[n, q]
        put(n, q, res * re, res * im)

    def e4(n, q, re, im):
        wr, wi = wave[n, 0, q], wave[n, 1, q]
        g[n, 2, q] = wr * re + wi * im
        g[n, 3, q] = wr * im - wi * re
        a, b = pick(n, 2, q), pick(n, 3, q)
        v[n, q] = (a * re + b * im).astype(BF16)
        v[n, moved(q, W)] = (a * im - b * re).astype(BF16)
    sweep(second_exit, transform(u, fwd_t, inv_t, e3), transform(u, inv_t, fwd_t, e4))

    def place(plane, _):
        for p, q in enumerate(PARTS):
            for o, f in enumerate(PARTS):
                row = lax.broadcasted_iota(jnp.int32, (H, H), 0) + q.start
                col = lax.broadcasted_iota(jnp.int32, (H, H), 1) + f.start
                every = upper = fore = both = None
                for n in range(NP):
                    x = g[n, plane, q, f]
                    x_up = jnp.where(row >= pos[0, n], x, 0.0)
                    x_fore = jnp.where(col >= pos[1, n], x, 0.0)
                    x_both = jnp.where(col >= pos[1, n], x_up, 0.0)
                    if n == 0:
                        every, upper, fore, both = x, x_up, x_fore, x_both
                    else:
                        every, upper, fore, both = every + x, upper + x_up, fore + x_fore, both + x_both
                back_up = upper - both
                down_fore = fore - both
                parts = {(0, 0): both, (0, 1): back_up, (1, 0): down_fore, (1, 1): every - fore - back_up}
                for (a, b), val in parts.items():
                    j = 2 * b + o
                    if a == p:
                        out_row[a, plane, :, j * H:(j + 1) * H] = val.astype(BF16)
                    else:
                        rows = slice(a * H, (a + 1) * H)
                        if b == o:
                            out_col[b, plane, rows] = val.astype(BF16)
                        else:
                            center[plane, rows, b * H:(b + 1) * H] = val
        return 0

    def add_fold(s, k):
        dr, dc = AROUND[k]
        e = half_of(-dr)
        f = half_of(-dc)

        @pl.when(lands(k))
        def _():
            fold(s, k).wait_recv()
            for plane in (2 * s, 2 * s + 1):
                if dr:
                    got = got_row[0 if dr < 0 else 1, plane, :, spot_of(dc)]
                else:
                    got = got_col[0 if dc < 0 else 1, plane]
                center[plane, e, f] += got.astype(F32)

    lax.fori_loop(2, 4, place, 0)
    fold_start(1)


    def e5(n, q, re, im):
        p, t = prop[0, q], prop[1, q]
        put(n, q, p * re + t * im, p * im - t * re)

    def e6(n, q, re, im):
        p, t = pr[n, 0, q], pr[n, 1, q]
        g[n, 0, q] = p * re + t * im
        g[n, 1, q] = p * im - t * re
        a, b = pick(n, 0, q), pick(n, 1, q)
        wave[n, 0, q] = a * re + b * im
        wave[n, 1, q] = a * im - b * re

    def probe_back(n):
        sums[0] += back(wave[n, 0], n)
        sums[1] += back(wave[n, 1], n)
    last = transform(u, inv_t, fwd_t, e6)

    def last_and_back(n):
        last(n)
        probe_back(n)
    sweep(transform(v, fwd_t, inv_t, e5), last_and_back)

    mine = pl.ds(pl.multiple_of(core * H, H), H)
    other = pl.ds(pl.multiple_of((1 - core) * H, H), H)
    core_out[...] = sums[:, other].astype(BF16)
    swap = to_mate(core_out, core_got, 0, mates[0])
    swap.start()
    fold_turn(1)
    lax.fori_loop(0, 2, place, 0)
    fold_start(0)

    Q = H // XS
    swap.wait()
    sums[:, mine] = sums[:, mine] + core_got[...].astype(F32)
    spread = []
    for d in range(1, XS):
        at = pl.multiple_of(core * H + lax.rem(xi + d, XS) * Q, Q)
        x_out[d - 1] = sums[:, pl.ds(at, Q)].astype(BF16)
        cp = to_mate(x_out.at[d - 1], x_got.at[d - 1], d, mates[1 + d])
        cp.start()
        spread.append(cp)
    acc = sums[:, pl.ds(pl.multiple_of(core * H + xi * Q, Q), Q)]
    for d in range(1, XS):
        spread[d - 1].wait()
        acc = acc + x_got[d - 1].astype(F32)
    z_out[...] = acc.astype(BF16)
    cross = to_mate(z_out, z_got, XS, mates[1])
    cross.start()
    fold_turn(0)
    for k in range(8):
        add_fold(1, k)
    cross.wait()
    tot = z_out[...].astype(F32) + z_got[...].astype(F32)
    scale = 1.0 / jnp.sqrt(tot[2] + 1e-06)
    here = pl.ds(pl.multiple_of(core * H + xi * Q, Q), Q)
    fin[0, here] = (tot[0] * scale).astype(BF16)
    fin[1, here] = (tot[1] * scale).astype(BF16)
    gather = []
    for i, mate in enumerate(mates[2:] + crossed + mates[:1]):
        cp = to_mate(fin.at[:, here], fin.at[:, here], XS + 1 + i, mate)
        cp.start()
        gather.append(cp)
    for k in (6, 7, 0, 1, 2, 3, 4, 5):
        add_fold(0, k)
    for cp in gather:
        cp.wait()
    for s in range(2):
        halo_sent(s)
        fold_sent(s)


def finish_kernel(grad, probe, grad_out, probe_out, sem):
    put = pltpu.make_async_copy(grad, grad_out, sem)
    put.start()
    for k in range(2):
        probe_out[k] = probe[k].astype(F32)
    put.wait()


def tables():
    k = np.arange(W)
    ang = 2.0 * np.pi * ((k[:, None] * k[None, :]) % W) / W
    both = np.stack([np.cos(ang), np.sin(ang)]) / np.sqrt(W)
    return jnp.asarray(both.astype(np.float32)).astype(BF16)


def on_device(n_row, n_col, object_slices, probe_wave_parts, prop_phase, measured, positions):
    vm = pl.BlockSpec(memory_space=pltpu.VMEM)
    anys = pl.BlockSpec(memory_space=pl.ANY)
    shape = jax.ShapeDtypeStruct
    Q = H // XS
    dma = pltpu.SemaphoreType.DMA
    grad, probe_grad = pl.pallas_call(
        functools.partial(kernel, n_row, n_col),
        out_shape=(pltpu.VMEM((4, W, W), F32), pltpu.VMEM((2, W, W), BF16)),
        in_specs=[pl.BlockSpec(memory_space=pltpu.SMEM)] + [anys] * 5,
        out_specs=(vm, vm),
        scratch_shapes=[
            pltpu.VMEM((2, W, W), F32), pltpu.VMEM((W, W), F32), pltpu.VMEM((2, W, W), BF16),
            pltpu.VMEM((2 * W, 2 * W), BF16), pltpu.VMEM((2 * W, 2 * W), BF16), pltpu.VMEM((2, W, W), F32),
            pltpu.VMEM((NP, 2 * W, W), BF16), pltpu.VMEM((NP, 2 * W, W), BF16), pltpu.VMEM((NP, W, 2 * W), BF16),
            pltpu.VMEM((4, 2 * W, 2 * W), BF16), pltpu.VMEM((NP, 2, W, W), F32), pltpu.VMEM((NP, 2, W, W), F32),
            pltpu.VMEM((NP, 4, W, W), F32), pltpu.VMEM((3, W, W), F32), pltpu.VMEM((NP, W, W), F32),
            pltpu.VMEM((2, 4, H, 2 * W), BF16), pltpu.VMEM((2, 4, W, H), BF16),
            pltpu.VMEM((2, 4, H, 2 * W), BF16), pltpu.VMEM((2, 4, W, H), BF16),
            pltpu.VMEM((3, H, W), BF16), pltpu.VMEM((3, H, W), BF16),
            pltpu.VMEM((XS - 1, 3, Q, W), BF16), pltpu.VMEM((XS - 1, 3, Q, W), BF16),
            pltpu.VMEM((3, Q, W), BF16), pltpu.VMEM((3, Q, W), BF16),
            pltpu.VMEM((2, 4, 2, H, H), BF16), dma((5,)), dma((2, 4)), dma((2, 4)), dma((2, 8)), dma((2, 8)), dma((2, 8)), dma((2, 8)), dma((3 * XS,)), dma((3 * XS,)),
        ],
        compiler_params=pltpu.CompilerParams(collective_id=0, has_side_effects=True, vmem_limit_bytes=60 << 20),
    )(positions.T, object_slices.reshape(4, W, W), probe_wave_parts[0], prop_phase, measured, tables())
    grad_out, probe_out = pl.pallas_call(
        finish_kernel,
        out_shape=(shape((4, W, W), F32), shape((2, W, W), F32)),
        in_specs=[vm, vm],
        out_specs=(anys, vm),
        scratch_shapes=[dma],
    )(pltpu.with_memory_space_constraint(grad, pltpu.VMEM), pltpu.with_memory_space_constraint(probe_grad, pltpu.VMEM))
    return grad_out.reshape(2, 2, W, W), probe_out[None]


def solution(mesh):
    return jax.shard_map(
        functools.partial(on_device, mesh.shape["row"], mesh.shape["col"]),
        mesh=mesh,
        in_specs=(
            P(None, None, "row", "col"),
            P("col", None, None, None),
            P(),
            P(("row", "col"), None, None),
            P(("row", "col"), None),
        ),
        out_specs=(P(None, None, "row", "col"), P("col", None, None, None)),
        check_vma=False,
    )
```

```python
import functools

import jax
import jax.numpy as jnp
import numpy as np
from jax import lax
from jax.experimental import pallas as pl
from jax.experimental.pallas import tpu as pltpu
from jax.sharding import PartitionSpec as P

W = 256
H = 128
NP = 4
RC = 128
UNROLL = 4
F32, BF16 = jnp.float32, jnp.bfloat16
MESH = pl.DeviceIdType.MESH
AROUND = ((-1, 0), (1, 0), (-1, -1), (-1, 1), (1, -1), (1, 1), (0, -1), (0, 1))
CHUNKS = [slice(i, i + RC) for i in range(0, W, RC)]
PARTS = [slice(0, H), slice(H, W)]
XS, ZS = 4, 2
LOOP = 8
TURNS = [(dr, dc) for dc in (-1, 1) for dr in (-1, 1)]


def half_of(step):
    return {-1: slice(0, H), 0: slice(0, W), 1: slice(H, W)}[step]


def rim_of(step):
    return {-1: slice(3 * H, 4 * H), 0: slice(H, 3 * H), 1: slice(0, H)}[step]


def spot_of(step):
    return {-1: slice(0, H), 0: slice(H, 3 * H), 1: slice(3 * H, 4 * H)}[step]


def moved(q, by):
    return slice(q.start + by, q.stop + by)


def kernel(
    n_row, n_col,
    pos, obj, probe_in, phase_in, meas_in, cs_in,
    center, fin,
    probe, phase, cs, fwd_t, inv_t, prop, u, v, h, ext, pr, wave, g, sums, meas,
    out_row, out_col, got_row, got_col,
    core_out, core_got, x_out, x_got, z_out, z_got,
    turned, local_sem, turn_send, turn_recv, halo_send, halo_recv, fold_send, fold_recv, sum_send, sum_recv,
):
    r, c = lax.axis_index("row"), lax.axis_index("col")
    core = lax.rem(r, 2)
    xi = lax.rem(r // 2, XS)
    zi = r // (2 * XS)

    def inside(dr, dc):
        ok = None
        for idx, step, count in ((r, dr, n_row), (c, dc, n_col)):
            if step:
                here = (idx > 0) if step < 0 else (idx < count - 1)
                ok = here if ok is None else ok & here
        return ok

    def col_far(at, step):
        return lax.rem(at, LOOP) == (LOOP - 1 if step > 0 else 0)

    def row_far(at, step):
        return at == (n_row // ZS - 1 if step > 0 else n_row // ZS)

    def bent(row, col, dr, dc):
        return col_far(col, dc) & jnp.logical_not(row_far(row, dr))

    def leaves(k):
        dr, dc = AROUND[k]
        ok = inside(dr, dc)
        return ok & jnp.logical_not(bent(r, c, dr, dc)) if dr and dc else ok

    def lands(k):
        dr, dc = AROUND[k]
        ok = inside(-dr, -dc)
        return ok & jnp.logical_not(bent(r - dr, c - dc, dr, dc)) if dr and dc else ok

    def row_at(z, x, k):
        return (z * XS + x) * 2 + k

    mates = [(row_at(zi, xi, 1 - core), c), (row_at(1 - zi, xi, core), c)]
    mates += [(row_at(zi, lax.rem(xi + d, XS), core), c) for d in range(1, XS)]

    crossed = [(row_at(zi, lax.rem(xi + d, XS), 1 - core), c) for d in range(1, XS)]

    barrier = pltpu.get_barrier_semaphore()
    for dr, dc in AROUND:
        @pl.when(inside(dr, dc))
        def _():
            pl.semaphore_signal(barrier, inc=1, device_id=(r + dr, c + dc), device_id_type=MESH)
    for mate in mates[1:] + crossed:
        pl.semaphore_signal(barrier, inc=1, device_id=mate, device_id_type=MESH)
    own = pltpu.make_async_copy(obj, ext.at[:, pl.ds(H, W), pl.ds(H, W)], local_sem.at[0])
    own.start()
    load = pltpu.make_async_copy(meas_in, meas, local_sem.at[1])
    load.start()
    small = [
        pltpu.make_async_copy(a, b, local_sem.at[2 + i])
        for i, (a, b) in enumerate(((probe_in, probe), (phase_in, phase), (cs_in, cs)))
    ]
    for cp in small:
        cp.start()
    peers = jnp.int32(len(mates) - 1 + len(crossed))
    for dr, dc in AROUND:
        peers = peers + inside(dr, dc).astype(jnp.int32)
    pl.semaphore_wait(barrier, peers)

    def halo(s, k):
        dr, dc = AROUND[k]
        a, b, e, f = half_of(dr), half_of(dc), rim_of(dr), rim_of(dc)
        return pltpu.make_async_remote_copy(
            src_ref=obj.at[pl.ds(2 * s, 2), a, b],
            dst_ref=ext.at[pl.ds(2 * s, 2), e, f],
            send_sem=halo_send.at[s, k],
            recv_sem=halo_recv.at[s, k],
            device_id=(r + dr, c + dc),
            device_id_type=MESH,
        )

    def fold(s, k):
        dr, dc = AROUND[k]
        if dr:
            i = 0 if dr < 0 else 1
            place = (i, pl.ds(2 * s, 2), slice(None), spot_of(dc))
            src, dst = out_row.at[place], got_row.at[place]
        else:
            i = 0 if dc < 0 else 1
            place = (i, pl.ds(2 * s, 2))
            src, dst = out_col.at[place], got_col.at[place]
        return pltpu.make_async_remote_copy(
            src_ref=src, dst_ref=dst, send_sem=fold_send.at[s, k], recv_sem=fold_recv.at[s, k],
            device_id=(r + dr, c + dc), device_id_type=MESH,
        )

    def to_mate(src, dst, i, mate):
        return pltpu.make_async_remote_copy(
            src_ref=src, dst_ref=dst, send_sem=sum_send.at[i], recv_sem=sum_recv.at[i],
            device_id=mate, device_id_type=MESH,
        )

    def pass_on(s, t):
        dr, dc = TURNS[t]
        e, f = half_of(dr), rim_of(dc)
        return pltpu.make_async_remote_copy(
            src_ref=ext.at[pl.ds(2 * s, 2), moved(e, H), f],
            dst_ref=ext.at[pl.ds(2 * s, 2), rim_of(dr), f],
            send_sem=turn_send.at[s, t],
            recv_sem=halo_recv.at[s, AROUND.index((dr, dc))],
            device_id=(r + dr, c),
            device_id_type=MESH,
        )

    def turn(s, t):
        dr, dc = TURNS[t]
        k = AROUND.index((dr, dc))
        place = (0 if dr < 0 else 1, pl.ds(2 * s, 2), slice(None), spot_of(dc))
        return pltpu.make_async_remote_copy(
            src_ref=out_row.at[place], dst_ref=turned.at[s, t], send_sem=fold_send.at[s, k], recv_sem=turn_recv.at[s, t],
            device_id=(r + dr, c), device_id_type=MESH,
        )

    def passes(t):
        dr, dc = TURNS[t]
        return inside(0, -dc) & inside(dr, 0) & bent(r, c - dc, dr, dc)

    def gets(t):
        dr, dc = TURNS[t]
        return inside(0, dc) & inside(-dr, 0) & bent(r - dr, c, dr, dc)

    def halo_start(s):
        for k in range(8):
            @pl.when(leaves(k))
            def _():
                halo(s, k).start()

    def halo_turn(s):
        for dc in (-1, 1):
            @pl.when(inside(0, -dc) & col_far(c - dc, dc))
            def _():
                halo(s, AROUND.index((0, dc))).wait_recv()
        for t in range(4):
            @pl.when(passes(t))
            def _():
                pass_on(s, t).start()

    def halo_arrived(s):
        for k, (dr, dc) in enumerate(AROUND):
            ok = inside(-dr, -dc)
            if not dr:
                ok = ok & jnp.logical_not(col_far(c - dc, dc))

            @pl.when(ok)
            def _():
                halo(s, k).wait_recv()

    def halo_sent(s):
        for k in range(8):
            @pl.when(leaves(k))
            def _():
                halo(s, k).wait_send()
        for t in range(4):
            @pl.when(passes(t))
            def _():
                pass_on(s, t).wait_send()

    def fold_start(s):
        for k, (dr, dc) in enumerate(AROUND):
            ok = leaves(k)
            if not dr:
                ok = ok & jnp.logical_not(col_far(c, dc))
            elif dc:
                @pl.when(inside(dr, dc) & bent(r, c, dr, dc))
                def _():
                    turn(s, TURNS.index((dr, dc))).start()

            @pl.when(ok)
            def _():
                fold(s, k).start()

    def fold_turn(s):
        for t, (dr, dc) in enumerate(TURNS):
            @pl.when(gets(t))
            def _():
                turn(s, t).wait_recv()
                rows = half_of(-dr)
                for p in range(2):
                    i = (0 if dc < 0 else 1, 2 * s + p, rows)
                    out_col[i] = (out_col[i].astype(F32) + turned[s, t, p].astype(F32)).astype(BF16)
        for dc in (-1, 1):
            @pl.when(inside(0, dc) & col_far(c, dc))
            def _():
                fold(s, AROUND.index((0, dc))).start()

    def fold_sent(s):
        for k, (dr, dc) in enumerate(AROUND):
            @pl.when(inside(dr, dc))
            def _():
                fold(s, k).wait_send()

    halo_start(0)
    halo_start(1)

    for dr, dc in AROUND:
        @pl.when(jnp.logical_not(inside(-dr, -dc)))
        def _():
            e, f = rim_of(dr), rim_of(dc)
            ext[:, e, f] = jnp.zeros((4, e.stop - e.start, f.stop - f.start), BF16)

    for cp in small:
        cp.wait()
    cos_t, sin_t = cs[0], cs[1]
    for t, sgn in ((fwd_t, 1), (inv_t, -1)):
        t[0:W, 0:W] = cos_t
        t[W:, W:] = cos_t
        t[0:W, W:] = sin_t if sgn > 0 else -sin_t
        t[W:, 0:W] = -sin_t if sgn > 0 else sin_t
    for q in CHUNKS:
        prop[0, q] = jnp.cos(phase[q])
        prop[1, q] = jnp.sin(phase[q])
    sums[...] = jnp.zeros_like(sums)

    def rolled(n, _):
        for k in range(2):
            pr[n, k] = pltpu.roll(pltpu.roll(probe[k], pos[0, n], 0), pos[1, n], 1)
        return 0
    lax.fori_loop(0, NP, rolled, 0)

    def transform(src, lt, rt, epilogue):
        def run(n):
            half = jnp.dot(lt[...], src[n], preferred_element_type=F32)
            h[n, :, 0:W] = half[0:W].astype(BF16)
            h[n, :, W:] = half[W:].astype(BF16)
            for q in CHUNKS:
                o = jnp.dot(h[n, q, :], rt[...], preferred_element_type=F32)
                epilogue(n, q, o[:, 0:W], o[:, W:])
        return run

    def put(n, q, re, im):
        u[n, q, :] = re.astype(BF16)
        u[n, moved(q, W), :] = im.astype(BF16)

    def pick(n, plane, q):
        col = lax.broadcasted_iota(jnp.int32, (RC, W), 1) >= pos[1, n]
        row = lax.broadcasted_iota(jnp.int32, (RC, W), 0) + q.start >= pos[0, n]
        q2 = moved(q, W)
        a = jnp.where(col, ext[plane, q, 0:W].astype(F32), ext[plane, q, W:].astype(F32))
        b = jnp.where(col, ext[plane, q2, 0:W].astype(F32), ext[plane, q2, W:].astype(F32))
        return jnp.where(row, a, b)

    def sweep(*stages):
        def some(i, _):
            for stage in stages:
                for k in range(UNROLL):
                    stage(i * UNROLL + k)
            return 0
        if UNROLL == NP:
            some(0, 0)
        else:
            lax.fori_loop(0, NP // UNROLL, some, 0)

    def back(x, n):
        return pltpu.roll(pltpu.roll(x, W - pos[0, n], 0), W - pos[1, n], 1)

    halo_turn(0)
    Q = H // XS
    mine = pl.ds(pl.multiple_of(core * H, H), H)
    other = pl.ds(pl.multiple_of((1 - core) * H, H), H)
    GROUPS = (slice(0, 2), slice(2, 3))

    def swap_start(i):
        p = GROUPS[i]
        core_out[p] = sums[p, other].astype(BF16)
        cp = to_mate(core_out.at[p], core_got.at[p], i * (XS + 1), mates[0])
        cp.start()
        return cp

    def spread_start(i, cp):
        p = GROUPS[i]
        cp.wait()
        sums[p, mine] = sums[p, mine] + core_got[p].astype(F32)
        cps = []
        for d in range(1, XS):
            at = pl.multiple_of(core * H + lax.rem(xi + d, XS) * Q, Q)
            x_out[d - 1, p] = sums[p, pl.ds(at, Q)].astype(BF16)
            cps.append(to_mate(x_out.at[d - 1, p], x_got.at[d - 1, p], i * (XS + 1) + d, mates[1 + d]))
            cps[-1].start()
        return cps

    def cross_start(i, cps):
        p = GROUPS[i]
        acc = sums[p, pl.ds(pl.multiple_of(core * H + xi * Q, Q), Q)]
        for d in range(1, XS):
            cps[d - 1].wait()
            acc = acc + x_got[d - 1, p].astype(F32)
        z_out[p] = acc.astype(BF16)
        cp = to_mate(z_out.at[p], z_got.at[p], i * (XS + 1) + XS, mates[1])
        cp.start()
        return cp

    own.wait()
    halo_arrived(0)

    def first_exit(n):
        for q in CHUNKS:
            a, b = pick(n, 0, q), pick(n, 1, q)
            p, t = pr[n, 0, q], pr[n, 1, q]
            put(n, q, p * a - t * b, p * b + t * a)
            g[n, 0, q] = a * a + b * b

    def bright(n):
        sums[2] += back(g[n, 0], n)

    def e1(n, q, re, im):
        p, t = prop[0, q], prop[1, q]
        put(n, q, p * re - t * im, p * im + t * re)

    def e2(n, q, re, im):
        wave[n, 0, q] = re
        wave[n, 1, q] = im
    into_spectrum = transform(u, fwd_t, inv_t, e1)

    def spectrum(n):
        into_spectrum(n)
        bright(n)
    sweep(first_exit, spectrum)
    swap_light = swap_start(1)
    halo_turn(1)
    sweep(transform(u, inv_t, fwd_t, e2))

    load.wait()
    halo_arrived(1)

    def second_exit(n):
        for q in CHUNKS:
            a, b = pick(n, 2, q), pick(n, 3, q)
            re, im = wave[n, 0, q], wave[n, 1, q]
            put(n, q, re * a - im * b, re * b + im * a)

    def e3(n, q, re, im):
        res = re * re + im * im - meas[n, q]
        put(n, q, res * re, res * im)

    def e4(n, q, re, im):
        wr, wi = wave[n, 0, q], wave[n, 1, q]
        g[n, 2, q] = wr * re + wi * im
        g[n, 3, q] = wr * im - wi * re
        a, b = pick(n, 2, q), pick(n, 3, q)
        v[n, q] = (a * re + b * im).astype(BF16)
        v[n, moved(q, W)] = (a * im - b * re).astype(BF16)
    sweep(second_exit, transform(u, fwd_t, inv_t, e3), transform(u, inv_t, fwd_t, e4))

    def place(plane, _):
        for p, q in enumerate(PARTS):
            for o, f in enumerate(PARTS):
                row = lax.broadcasted_iota(jnp.int32, (H, H), 0) + q.start
                col = lax.broadcasted_iota(jnp.int32, (H, H), 1) + f.start
                every = upper = fore = both = None
                for n in range(NP):
                    x = g[n, plane, q, f]
                    x_up = jnp.where(row >= pos[0, n], x, 0.0)
                    x_fore = jnp.where(col >= pos[1, n], x, 0.0)
                    x_both = jnp.where(col >= pos[1, n], x_up, 0.0)
                    if n == 0:
                        every, upper, fore, both = x, x_up, x_fore, x_both
                    else:
                        every, upper, fore, both = every + x, upper + x_up, fore + x_fore, both + x_both
                back_up = upper - both
                down_fore = fore - both
                parts = {(0, 0): both, (0, 1): back_up, (1, 0): down_fore, (1, 1): every - fore - back_up}
                for (a, b), val in parts.items():
                    j = 2 * b + o
                    if a == p:
                        out_row[a, plane, :, j * H:(j + 1) * H] = val.astype(BF16)
                    else:
                        rows = slice(a * H, (a + 1) * H)
                        if b == o:
                            out_col[b, plane, rows] = val.astype(BF16)
                        else:
                            center[plane, rows, b * H:(b + 1) * H] = val
        return 0

    def add_fold(s, k):
        dr, dc = AROUND[k]
        e = half_of(-dr)
        f = half_of(-dc)

        @pl.when(lands(k))
        def _():
            fold(s, k).wait_recv()
            for plane in (2 * s, 2 * s + 1):
                if dr:
                    got = got_row[0 if dr < 0 else 1, plane, :, spot_of(dc)]
                else:
                    got = got_col[0 if dc < 0 else 1, plane]
                center[plane, e, f] += got.astype(F32)

    lax.fori_loop(2, 4, place, 0)
    fold_start(1)
    light = spread_start(1, swap_light)


    def e5(n, q, re, im):
        p, t = prop[0, q], prop[1, q]
        put(n, q, p * re + t * im, p * im - t * re)

    def e6(n, q, re, im):
        p, t = pr[n, 0, q], pr[n, 1, q]
        g[n, 0, q] = p * re + t * im
        g[n, 1, q] = p * im - t * re
        a, b = pick(n, 0, q), pick(n, 1, q)
        wave[n, 0, q] = a * re + b * im
        wave[n, 1, q] = a * im - b * re

    def probe_back(n):
        sums[0] += back(wave[n, 0], n)
        sums[1] += back(wave[n, 1], n)
    last = transform(u, inv_t, fwd_t, e6)

    def last_and_back(n):
        last(n)
        probe_back(n)
    sweep(transform(v, fwd_t, inv_t, e5))
    fold_turn(1)
    sweep(last_and_back)

    swap = swap_start(0)
    cross_light = cross_start(1, light)
    lax.fori_loop(0, 2, place, 0)
    fold_start(0)
    spread = spread_start(0, swap)
    cross = cross_start(0, spread)
    fold_turn(0)
    for k in range(8):
        add_fold(1, k)
    cross.wait()
    cross_light.wait()
    tot = z_out[...].astype(F32) + z_got[...].astype(F32)
    scale = 1.0 / jnp.sqrt(tot[2] + 1e-06)
    here = pl.ds(pl.multiple_of(core * H + xi * Q, Q), Q)
    fin[0, here] = (tot[0] * scale).astype(BF16)
    fin[1, here] = (tot[1] * scale).astype(BF16)
    gather = []
    for i, mate in enumerate(mates[2:] + crossed + mates[:1]):
        cp = to_mate(fin.at[:, here], fin.at[:, here], 2 * (XS + 1) + i, mate)
        cp.start()
        gather.append(cp)
    for k in (6, 7, 0, 1, 2, 3, 4, 5):
        add_fold(0, k)
    for cp in gather:
        cp.wait()
    for s in range(2):
        halo_sent(s)
        fold_sent(s)


def finish_kernel(grad, probe, grad_out, probe_out, sem):
    puts = [pltpu.make_async_copy(grad.at[k], grad_out.at[k], sem.at[k]) for k in range(4)]
    for put in puts:
        put.start()
    for k in range(2):
        probe_out[k] = probe[k].astype(F32)
    for put in puts:
        put.wait()


def tables():
    k = np.arange(W)
    ang = 2.0 * np.pi * ((k[:, None] * k[None, :]) % W) / W
    both = np.stack([np.cos(ang), np.sin(ang)]) / np.sqrt(W)
    return jnp.asarray(both.astype(np.float32)).astype(BF16)


def on_device(n_row, n_col, object_slices, probe_wave_parts, prop_phase, measured, positions):
    vm = pl.BlockSpec(memory_space=pltpu.VMEM)
    anys = pl.BlockSpec(memory_space=pl.ANY)
    shape = jax.ShapeDtypeStruct
    Q = H // XS
    dma = pltpu.SemaphoreType.DMA
    grad, probe_grad = pl.pallas_call(
        functools.partial(kernel, n_row, n_col),
        out_shape=(pltpu.VMEM((4, W, W), F32), pltpu.VMEM((2, W, W), BF16)),
        in_specs=[pl.BlockSpec(memory_space=pltpu.SMEM)] + [anys] * 5,
        out_specs=(vm, vm),
        scratch_shapes=[
            pltpu.VMEM((2, W, W), F32), pltpu.VMEM((W, W), F32), pltpu.VMEM((2, W, W), BF16),
            pltpu.VMEM((2 * W, 2 * W), BF16), pltpu.VMEM((2 * W, 2 * W), BF16), pltpu.VMEM((2, W, W), F32),
            pltpu.VMEM((NP, 2 * W, W), BF16), pltpu.VMEM((NP, 2 * W, W), BF16), pltpu.VMEM((NP, W, 2 * W), BF16),
            pltpu.VMEM((4, 2 * W, 2 * W), BF16), pltpu.VMEM((NP, 2, W, W), F32), pltpu.VMEM((NP, 2, W, W), F32),
            pltpu.VMEM((NP, 4, W, W), F32), pltpu.VMEM((3, W, W), F32), pltpu.VMEM((NP, W, W), F32),
            pltpu.VMEM((2, 4, H, 2 * W), BF16), pltpu.VMEM((2, 4, W, H), BF16),
            pltpu.VMEM((2, 4, H, 2 * W), BF16), pltpu.VMEM((2, 4, W, H), BF16),
            pltpu.VMEM((3, H, W), BF16), pltpu.VMEM((3, H, W), BF16),
            pltpu.VMEM((XS - 1, 3, Q, W), BF16), pltpu.VMEM((XS - 1, 3, Q, W), BF16),
            pltpu.VMEM((3, Q, W), BF16), pltpu.VMEM((3, Q, W), BF16),
            pltpu.VMEM((2, 4, 2, H, H), BF16), dma((5,)), dma((2, 4)), dma((2, 4)), dma((2, 8)), dma((2, 8)), dma((2, 8)), dma((2, 8)), dma((4 * XS + 1,)), dma((4 * XS + 1,)),
        ],
        compiler_params=pltpu.CompilerParams(collective_id=0, has_side_effects=True, vmem_limit_bytes=60 << 20),
    )(positions.T, object_slices.reshape(4, W, W), probe_wave_parts[0], prop_phase, measured, tables())
    grad_out, probe_out = pl.pallas_call(
        finish_kernel,
        out_shape=(shape((4, W, W), F32), shape((2, W, W), F32)),
        in_specs=[vm, vm],
        out_specs=(anys, vm),
        scratch_shapes=[dma((4,))],
    )(pltpu.with_memory_space_constraint(grad, pltpu.VMEM), pltpu.with_memory_space_constraint(probe_grad, pltpu.VMEM))
    return grad_out.reshape(2, 2, W, W), probe_out[None]


def solution(mesh):
    return jax.shard_map(
        functools.partial(on_device, mesh.shape["row"], mesh.shape["col"]),
        mesh=mesh,
        in_specs=(
            P(None, None, "row", "col"),
            P("col", None, None, None),
            P(),
            P(("row", "col"), None, None),
            P(("row", "col"), None),
        ),
        out_specs=(P(None, None, "row", "col"), P("col", None, None, None)),
        check_vma=False,
    )
```

```python
import functools

import jax
import jax.numpy as jnp
import numpy as np
from jax import lax
from jax.experimental import pallas as pl
from jax.experimental.pallas import tpu as pltpu
from jax.sharding import PartitionSpec as P

W = 256
H = 128
NP = 4
RC = 128
UNROLL = 4
F32, BF16 = jnp.float32, jnp.bfloat16
MESH = pl.DeviceIdType.MESH
AROUND = ((-1, 0), (1, 0), (-1, -1), (-1, 1), (1, -1), (1, 1), (0, -1), (0, 1))
CHUNKS = [slice(i, i + RC) for i in range(0, W, RC)]
PARTS = [slice(0, H), slice(H, W)]
XS, ZS = 4, 2
LOOP = 8
TURNS = [(dr, dc) for dc in (-1, 1) for dr in (-1, 1)]


def half_of(step):
    return {-1: slice(0, H), 0: slice(0, W), 1: slice(H, W)}[step]


def rim_of(step):
    return {-1: slice(3 * H, 4 * H), 0: slice(H, 3 * H), 1: slice(0, H)}[step]


def spot_of(step):
    return {-1: slice(0, H), 0: slice(H, 3 * H), 1: slice(3 * H, 4 * H)}[step]


def moved(q, by):
    return slice(q.start + by, q.stop + by)


def kernel(
    n_row, n_col,
    pos, obj, probe_in, phase_in, meas_in, cs_in,
    center, fin,
    probe, phase, cs, fwd_t, inv_t, prop, u, v, h, ext, pr, wave, g, sums, meas,
    out_row, out_col, got_row, got_col,
    core_out, core_got, x_out, x_got, z_out, z_got,
    turned, local_sem, turn_send, turn_recv, halo_send, halo_recv, fold_send, fold_recv, sum_send, sum_recv,
):
    r, c = lax.axis_index("row"), lax.axis_index("col")
    core = lax.rem(r, 2)
    xi = lax.rem(r // 2, XS)
    zi = r // (2 * XS)

    def inside(dr, dc):
        ok = None
        for idx, step, count in ((r, dr, n_row), (c, dc, n_col)):
            if step:
                here = (idx > 0) if step < 0 else (idx < count - 1)
                ok = here if ok is None else ok & here
        return ok

    def col_far(at, step):
        return lax.rem(at, LOOP) == (LOOP - 1 if step > 0 else 0)

    def row_far(at, step):
        return at == (n_row // ZS - 1 if step > 0 else n_row // ZS)

    def bent(row, col, dr, dc):
        return col_far(col, dc) & jnp.logical_not(row_far(row, dr))

    def leaves(k):
        dr, dc = AROUND[k]
        ok = inside(dr, dc)
        return ok & jnp.logical_not(bent(r, c, dr, dc)) if dr and dc else ok

    def lands(k):
        dr, dc = AROUND[k]
        ok = inside(-dr, -dc)
        return ok & jnp.logical_not(bent(r - dr, c - dc, dr, dc)) if dr and dc else ok

    def row_at(z, x, k):
        return (z * XS + x) * 2 + k

    mates = [(row_at(zi, xi, 1 - core), c), (row_at(1 - zi, xi, core), c)]
    mates += [(row_at(zi, lax.rem(xi + d, XS), core), c) for d in range(1, XS)]

    crossed = [(row_at(zi, lax.rem(xi + d, XS), 1 - core), c) for d in range(1, XS)]

    barrier = pltpu.get_barrier_semaphore()
    for dr, dc in AROUND:
        @pl.when(inside(dr, dc))
        def _():
            pl.semaphore_signal(barrier, inc=1, device_id=(r + dr, c + dc), device_id_type=MESH)
    for mate in mates[1:] + crossed:
        pl.semaphore_signal(barrier, inc=1, device_id=mate, device_id_type=MESH)
    own = pltpu.make_async_copy(obj, ext.at[:, pl.ds(H, W), pl.ds(H, W)], local_sem.at[0])
    own.start()
    load = pltpu.make_async_copy(meas_in, meas, local_sem.at[1])
    load.start()
    small = [
        pltpu.make_async_copy(a, b, local_sem.at[2 + i])
        for i, (a, b) in enumerate(((probe_in, probe), (phase_in, phase), (cs_in, cs)))
    ]
    for cp in small:
        cp.start()
    peers = jnp.int32(len(mates) - 1 + len(crossed))
    for dr, dc in AROUND:
        peers = peers + inside(dr, dc).astype(jnp.int32)
    pl.semaphore_wait(barrier, peers)

    def halo(s, k):
        dr, dc = AROUND[k]
        a, b, e, f = half_of(dr), half_of(dc), rim_of(dr), rim_of(dc)
        return pltpu.make_async_remote_copy(
            src_ref=obj.at[pl.ds(2 * s, 2), a, b],
            dst_ref=ext.at[pl.ds(2 * s, 2), e, f],
            send_sem=halo_send.at[s, k],
            recv_sem=halo_recv.at[s, k],
            device_id=(r + dr, c + dc),
            device_id_type=MESH,
        )

    def fold(s, k):
        dr, dc = AROUND[k]
        if dr:
            i = 0 if dr < 0 else 1
            place = (i, pl.ds(2 * s, 2), slice(None), spot_of(dc))
            src, dst = out_row.at[place], got_row.at[place]
        else:
            i = 0 if dc < 0 else 1
            place = (i, pl.ds(2 * s, 2))
            src, dst = out_col.at[place], got_col.at[place]
        return pltpu.make_async_remote_copy(
            src_ref=src, dst_ref=dst, send_sem=fold_send.at[s, k], recv_sem=fold_recv.at[s, k],
            device_id=(r + dr, c + dc), device_id_type=MESH,
        )

    def to_mate(src, dst, i, mate):
        return pltpu.make_async_remote_copy(
            src_ref=src, dst_ref=dst, send_sem=sum_send.at[i], recv_sem=sum_recv.at[i],
            device_id=mate, device_id_type=MESH,
        )

    def pass_on(s, t):
        dr, dc = TURNS[t]
        e, f = half_of(dr), rim_of(dc)
        return pltpu.make_async_remote_copy(
            src_ref=ext.at[pl.ds(2 * s, 2), moved(e, H), f],
            dst_ref=ext.at[pl.ds(2 * s, 2), rim_of(dr), f],
            send_sem=turn_send.at[s, t],
            recv_sem=halo_recv.at[s, AROUND.index((dr, dc))],
            device_id=(r + dr, c),
            device_id_type=MESH,
        )

    def turn(s, t):
        dr, dc = TURNS[t]
        k = AROUND.index((dr, dc))
        place = (0 if dr < 0 else 1, pl.ds(2 * s, 2), slice(None), spot_of(dc))
        return pltpu.make_async_remote_copy(
            src_ref=out_row.at[place], dst_ref=turned.at[s, t], send_sem=fold_send.at[s, k], recv_sem=turn_recv.at[s, t],
            device_id=(r + dr, c), device_id_type=MESH,
        )

    def passes(t):
        dr, dc = TURNS[t]
        return inside(0, -dc) & inside(dr, 0) & bent(r, c - dc, dr, dc)

    def gets(t):
        dr, dc = TURNS[t]
        return inside(0, dc) & inside(-dr, 0) & bent(r - dr, c, dr, dc)

    def halo_start(s):
        for k in range(8):
            @pl.when(leaves(k))
            def _():
                halo(s, k).start()

    def halo_turn(s):
        for dc in (-1, 1):
            @pl.when(inside(0, -dc) & col_far(c - dc, dc))
            def _():
                halo(s, AROUND.index((0, dc))).wait_recv()
        for t in range(4):
            @pl.when(passes(t))
            def _():
                pass_on(s, t).start()

    def halo_arrived(s):
        for k, (dr, dc) in enumerate(AROUND):
            ok = inside(-dr, -dc)
            if not dr:
                ok = ok & jnp.logical_not(col_far(c - dc, dc))

            @pl.when(ok)
            def _():
                halo(s, k).wait_recv()

    def halo_sent(s):
        for k in range(8):
            @pl.when(leaves(k))
            def _():
                halo(s, k).wait_send()
        for t in range(4):
            @pl.when(passes(t))
            def _():
                pass_on(s, t).wait_send()

    def fold_start(s):
        for k, (dr, dc) in enumerate(AROUND):
            ok = leaves(k)
            if not dr:
                ok = ok & jnp.logical_not(col_far(c, dc))
            elif dc:
                @pl.when(inside(dr, dc) & bent(r, c, dr, dc))
                def _():
                    turn(s, TURNS.index((dr, dc))).start()

            @pl.when(ok)
            def _():
                fold(s, k).start()

    def fold_turn(s):
        for t, (dr, dc) in enumerate(TURNS):
            @pl.when(gets(t))
            def _():
                turn(s, t).wait_recv()
                rows = half_of(-dr)
                for p in range(2):
                    i = (0 if dc < 0 else 1, 2 * s + p, rows)
                    out_col[i] = (out_col[i].astype(F32) + turned[s, t, p].astype(F32)).astype(BF16)
        for dc in (-1, 1):
            @pl.when(inside(0, dc) & col_far(c, dc))
            def _():
                fold(s, AROUND.index((0, dc))).start()

    def fold_sent(s):
        for k, (dr, dc) in enumerate(AROUND):
            @pl.when(inside(dr, dc))
            def _():
                fold(s, k).wait_send()

    halo_start(0)
    halo_start(1)

    for dr, dc in AROUND:
        @pl.when(jnp.logical_not(inside(-dr, -dc)))
        def _():
            e, f = rim_of(dr), rim_of(dc)
            ext[:, e, f] = jnp.zeros((4, e.stop - e.start, f.stop - f.start), BF16)

    for cp in small:
        cp.wait()
    cos_t, sin_t = cs[0], cs[1]
    for t, sgn in ((fwd_t, 1), (inv_t, -1)):
        t[0:W, 0:W] = cos_t
        t[W:, W:] = cos_t
        t[0:W, W:] = sin_t if sgn > 0 else -sin_t
        t[W:, 0:W] = -sin_t if sgn > 0 else sin_t
    for q in CHUNKS:
        prop[0, q] = jnp.cos(phase[q])
        prop[1, q] = jnp.sin(phase[q])
    sums[...] = jnp.zeros_like(sums)

    def rolled(n, _):
        for k in range(2):
            pr[n, k] = pltpu.roll(pltpu.roll(probe[k], pos[0, n], 0), pos[1, n], 1)
        return 0
    lax.fori_loop(0, NP, rolled, 0)

    def transform(src, lt, rt, epilogue):
        def run(n):
            half = jnp.dot(lt[...], src[n], preferred_element_type=F32)
            h[n, :, 0:W] = half[0:W].astype(BF16)
            h[n, :, W:] = half[W:].astype(BF16)
            for q in CHUNKS:
                o = jnp.dot(h[n, q, :], rt[...], preferred_element_type=F32)
                epilogue(n, q, o[:, 0:W], o[:, W:])
        return run

    def put(n, q, re, im):
        u[n, q, :] = re.astype(BF16)
        u[n, moved(q, W), :] = im.astype(BF16)

    def pick(n, plane, q):
        col = lax.broadcasted_iota(jnp.int32, (RC, W), 1) >= pos[1, n]
        row = lax.broadcasted_iota(jnp.int32, (RC, W), 0) + q.start >= pos[0, n]
        q2 = moved(q, W)
        a = jnp.where(col, ext[plane, q, 0:W].astype(F32), ext[plane, q, W:].astype(F32))
        b = jnp.where(col, ext[plane, q2, 0:W].astype(F32), ext[plane, q2, W:].astype(F32))
        return jnp.where(row, a, b)

    def sweep(*stages):
        def some(i, _):
            for stage in stages:
                for k in range(UNROLL):
                    stage(i * UNROLL + k)
            return 0
        if UNROLL == NP:
            some(0, 0)
        else:
            lax.fori_loop(0, NP // UNROLL, some, 0)

    def back(x, n):
        return pltpu.roll(pltpu.roll(x, W - pos[0, n], 0), W - pos[1, n], 1)

    halo_turn(0)
    own.wait()
    halo_arrived(0)

    def first_exit(n):
        for q in CHUNKS:
            a, b = pick(n, 0, q), pick(n, 1, q)
            p, t = pr[n, 0, q], pr[n, 1, q]
            put(n, q, p * a - t * b, p * b + t * a)
            g[n, 0, q] = a * a + b * b

    def bright(n):
        sums[2] += back(g[n, 0], n)

    def e1(n, q, re, im):
        p, t = prop[0, q], prop[1, q]
        put(n, q, p * re - t * im, p * im + t * re)

    def e2(n, q, re, im):
        wave[n, 0, q] = re
        wave[n, 1, q] = im
    into_spectrum = transform(u, fwd_t, inv_t, e1)

    def spectrum(n):
        into_spectrum(n)
        bright(n)
    sweep(first_exit, spectrum)
    halo_turn(1)
    sweep(transform(u, inv_t, fwd_t, e2))

    load.wait()
    halo_arrived(1)

    def second_exit(n):
        for q in CHUNKS:
            a, b = pick(n, 2, q), pick(n, 3, q)
            re, im = wave[n, 0, q], wave[n, 1, q]
            put(n, q, re * a - im * b, re * b + im * a)

    def e3(n, q, re, im):
        res = re * re + im * im - meas[n, q]
        put(n, q, res * re, res * im)

    def e4(n, q, re, im):
        wr, wi = wave[n, 0, q], wave[n, 1, q]
        g[n, 2, q] = wr * re + wi * im
        g[n, 3, q] = wr * im - wi * re
        a, b = pick(n, 2, q), pick(n, 3, q)
        v[n, q] = (a * re + b * im).astype(BF16)
        v[n, moved(q, W)] = (a * im - b * re).astype(BF16)
    sweep(second_exit, transform(u, fwd_t, inv_t, e3), transform(u, inv_t, fwd_t, e4))

    def place(plane, _):
        for p, q in enumerate(PARTS):
            for o, f in enumerate(PARTS):
                row = lax.broadcasted_iota(jnp.int32, (H, H), 0) + q.start
                col = lax.broadcasted_iota(jnp.int32, (H, H), 1) + f.start
                every = upper = fore = both = None
                for n in range(NP):
                    x = g[n, plane, q, f]
                    x_up = jnp.where(row >= pos[0, n], x, 0.0)
                    x_fore = jnp.where(col >= pos[1, n], x, 0.0)
                    x_both = jnp.where(col >= pos[1, n], x_up, 0.0)
                    if n == 0:
                        every, upper, fore, both = x, x_up, x_fore, x_both
                    else:
                        every, upper, fore, both = every + x, upper + x_up, fore + x_fore, both + x_both
                back_up = upper - both
                down_fore = fore - both
                parts = {(0, 0): both, (0, 1): back_up, (1, 0): down_fore, (1, 1): every - fore - back_up}
                for (a, b), val in parts.items():
                    j = 2 * b + o
                    if a == p:
                        out_row[a, plane, :, j * H:(j + 1) * H] = val.astype(BF16)
                    else:
                        rows = slice(a * H, (a + 1) * H)
                        if b == o:
                            out_col[b, plane, rows] = val.astype(BF16)
                        else:
                            center[plane, rows, b * H:(b + 1) * H] = val
        return 0

    def add_fold(s, k):
        dr, dc = AROUND[k]
        e = half_of(-dr)
        f = half_of(-dc)

        @pl.when(lands(k))
        def _():
            fold(s, k).wait_recv()
            for plane in (2 * s, 2 * s + 1):
                if dr:
                    got = got_row[0 if dr < 0 else 1, plane, :, spot_of(dc)]
                else:
                    got = got_col[0 if dc < 0 else 1, plane]
                center[plane, e, f] += got.astype(F32)

    lax.fori_loop(2, 4, place, 0)
    fold_start(1)


    def e5(n, q, re, im):
        p, t = prop[0, q], prop[1, q]
        put(n, q, p * re + t * im, p * im - t * re)

    def e6(n, q, re, im):
        p, t = pr[n, 0, q], pr[n, 1, q]
        g[n, 0, q] = p * re + t * im
        g[n, 1, q] = p * im - t * re
        a, b = pick(n, 0, q), pick(n, 1, q)
        wave[n, 0, q] = a * re + b * im
        wave[n, 1, q] = a * im - b * re

    def probe_back(n):
        sums[0] += back(wave[n, 0], n)
        sums[1] += back(wave[n, 1], n)
    last = transform(u, inv_t, fwd_t, e6)

    def last_and_back(n):
        last(n)
        probe_back(n)
    sweep(transform(v, fwd_t, inv_t, e5), last_and_back)

    mine = pl.ds(pl.multiple_of(core * H, H), H)
    other = pl.ds(pl.multiple_of((1 - core) * H, H), H)
    core_out[...] = sums[:, other].astype(BF16)
    swap = to_mate(core_out, core_got, 0, mates[0])
    swap.start()
    lax.fori_loop(0, 2, place, 0)
    fold_start(0)
    fold_turn(1)

    Q = H // XS
    swap.wait()
    sums[:, mine] = sums[:, mine] + core_got[...].astype(F32)
    spread = []
    for d in range(1, XS):
        at = pl.multiple_of(core * H + lax.rem(xi + d, XS) * Q, Q)
        x_out[d - 1] = sums[:, pl.ds(at, Q)].astype(BF16)
        cp = to_mate(x_out.at[d - 1], x_got.at[d - 1], d, mates[1 + d])
        cp.start()
        spread.append(cp)
    acc = sums[:, pl.ds(pl.multiple_of(core * H + xi * Q, Q), Q)]
    for d in range(1, XS):
        spread[d - 1].wait()
        acc = acc + x_got[d - 1].astype(F32)
    z_out[...] = acc.astype(BF16)
    cross = to_mate(z_out, z_got, XS, mates[1])
    cross.start()
    fold_turn(0)
    for k in range(8):
        add_fold(1, k)
    cross.wait()
    tot = z_out[...].astype(F32) + z_got[...].astype(F32)
    scale = 1.0 / jnp.sqrt(tot[2] + 1e-06)
    here = pl.ds(pl.multiple_of(core * H + xi * Q, Q), Q)
    fin[0, here] = (tot[0] * scale).astype(BF16)
    fin[1, here] = (tot[1] * scale).astype(BF16)
    gather = []
    for i, mate in enumerate(mates[2:] + crossed + mates[:1]):
        cp = to_mate(fin.at[:, here], fin.at[:, here], XS + 1 + i, mate)
        cp.start()
        gather.append(cp)
    for k in (6, 7, 0, 1, 2, 3, 4, 5):
        add_fold(0, k)
    for cp in gather:
        cp.wait()
    for s in range(2):
        halo_sent(s)
        fold_sent(s)


def finish_kernel(grad, probe, grad_out, probe_out, sem):
    put = pltpu.make_async_copy(grad, grad_out, sem)
    put.start()
    for k in range(2):
        probe_out[k] = probe[k].astype(F32)
    put.wait()


def tables():
    k = np.arange(W)
    ang = 2.0 * np.pi * ((k[:, None] * k[None, :]) % W) / W
    both = np.stack([np.cos(ang), np.sin(ang)]) / np.sqrt(W)
    return jnp.asarray(both.astype(np.float32)).astype(BF16)


def on_device(n_row, n_col, object_slices, probe_wave_parts, prop_phase, measured, positions):
    vm = pl.BlockSpec(memory_space=pltpu.VMEM)
    anys = pl.BlockSpec(memory_space=pl.ANY)
    shape = jax.ShapeDtypeStruct
    Q = H // XS
    dma = pltpu.SemaphoreType.DMA
    grad, probe_grad = pl.pallas_call(
        functools.partial(kernel, n_row, n_col),
        out_shape=(pltpu.VMEM((4, W, W), F32), pltpu.VMEM((2, W, W), BF16)),
        in_specs=[pl.BlockSpec(memory_space=pltpu.SMEM)] + [anys] * 5,
        out_specs=(vm, vm),
        scratch_shapes=[
            pltpu.VMEM((2, W, W), F32), pltpu.VMEM((W, W), F32), pltpu.VMEM((2, W, W), BF16),
            pltpu.VMEM((2 * W, 2 * W), BF16), pltpu.VMEM((2 * W, 2 * W), BF16), pltpu.VMEM((2, W, W), F32),
            pltpu.VMEM((NP, 2 * W, W), BF16), pltpu.VMEM((NP, 2 * W, W), BF16), pltpu.VMEM((NP, W, 2 * W), BF16),
            pltpu.VMEM((4, 2 * W, 2 * W), BF16), pltpu.VMEM((NP, 2, W, W), F32), pltpu.VMEM((NP, 2, W, W), F32),
            pltpu.VMEM((NP, 4, W, W), F32), pltpu.VMEM((3, W, W), F32), pltpu.VMEM((NP, W, W), F32),
            pltpu.VMEM((2, 4, H, 2 * W), BF16), pltpu.VMEM((2, 4, W, H), BF16),
            pltpu.VMEM((2, 4, H, 2 * W), BF16), pltpu.VMEM((2, 4, W, H), BF16),
            pltpu.VMEM((3, H, W), BF16), pltpu.VMEM((3, H, W), BF16),
            pltpu.VMEM((XS - 1, 3, Q, W), BF16), pltpu.VMEM((XS - 1, 3, Q, W), BF16),
            pltpu.VMEM((3, Q, W), BF16), pltpu.VMEM((3, Q, W), BF16),
            pltpu.VMEM((2, 4, 2, H, H), BF16), dma((5,)), dma((2, 4)), dma((2, 4)), dma((2, 8)), dma((2, 8)), dma((2, 8)), dma((2, 8)), dma((3 * XS,)), dma((3 * XS,)),
        ],
        compiler_params=pltpu.CompilerParams(collective_id=0, has_side_effects=True, vmem_limit_bytes=60 << 20),
    )(positions.T, object_slices.reshape(4, W, W), probe_wave_parts[0], prop_phase, measured, tables())
    grad_out, probe_out = pl.pallas_call(
        finish_kernel,
        out_shape=(shape((4, W, W), F32), shape((2, W, W), F32)),
        in_specs=[vm, vm],
        out_specs=(anys, vm),
        scratch_shapes=[dma],
    )(pltpu.with_memory_space_constraint(grad, pltpu.VMEM), pltpu.with_memory_space_constraint(probe_grad, pltpu.VMEM))
    return grad_out.reshape(2, 2, W, W), probe_out[None]


def solution(mesh):
    return jax.shard_map(
        functools.partial(on_device, mesh.shape["row"], mesh.shape["col"]),
        mesh=mesh,
        in_specs=(
            P(None, None, "row", "col"),
            P("col", None, None, None),
            P(),
            P(("row", "col"), None, None),
            P(("row", "col"), None),
        ),
        out_specs=(P(None, None, "row", "col"), P("col", None, None, None)),
        check_vma=False,
    )
```
